32 devices in a mesh: cohort: 8 (over z, y), stripe: 4 (over x, core).
Axes of the slice: x: 2, y: 2, z: 4, core: 2. Of those that a mesh axis runs over, the one named last changes fastest.
Arguments:
- cohort_scores: bfloat16 [8, 18432, 256], P('cohort', 'stripe'), may hold values from -6 to 6
- allele_match: int32 [8, 18432], P('cohort', 'stripe'), may hold values from 0 to 18431, as said below
- allele_flip: int32 [8, 18432], P('cohort', 'stripe'), may hold values 0 or 1
- precision: float32 [8, 18432], P('cohort', 'stripe'), may hold values from 0.3 to 900
- reference_panel: bfloat16 [512, 18432], P(None, 'stripe'), may hold values from -20 to 20
- gene_weights: bfloat16 [64, 49, 4608], P('stripe'), may hold values from -0.09375 to 0.09375
- window_start: int32 [64], P('stripe'), may hold values from 0 to 17856, as said below
- window_length: int32 [64], P('stripe'), may hold values from 576 to 4608
Outputs:
- association: float32 [64, 49, 256], P('stripe', None, 'cohort')
The draws below stay inside these ranges and needn't reach their ends.
Inputs may be any that keep to these rules, and one draw needn't show every extreme that they name: `allele_match`: within each cohort every variant is matched by exactly one row. The 4608 rows of one device match exactly 1152 variants of each stripe, stripe s being variants s * 4608 to (s + 1) * 4608 - 1. `window_start`: genes 16 * s to 16 * (s + 1) - 1 have their window start in stripe s; every window ends within the 18432 variants.
All inputs are finite; a program needn't handle non-finite values. No bound on the sum of `allele_flip` on one device may be relied on, other than what follows from the above.
Results may differ from the reference program's by a relative error of at most 0.004.
Values may be sent and summed in bfloat16 or wider, within the bound.
A program may use at most 128 MiB of HBM per device.

```python
import math
import jax
import jax.numpy as jnp
from jax import lax

ROWS = 4608
GENES_DEV = 16
TRAITS = 256
TISSUES = 49
N_REF = 512
L_MAX = 4608
COHORTS = 8
STRIPES = 4
VARIANTS = 18432
GENES = 64


def draw_allele_match(key, part):
    cohort_keys = jax.random.split(key, COHORTS)

    def one_cohort(cohort_key):
        first_key, second_key = jax.random.split(cohort_key)
        orders = jax.vmap(lambda stripe_key: jax.random.permutation(stripe_key, ROWS))(jax.random.split(first_key, STRIPES))
        global_index = orders.astype(jnp.int32) + (jnp.arange(STRIPES, dtype=jnp.int32) * ROWS)[:, None]
        by_source = global_index.reshape(STRIPES, STRIPES, ROWS // STRIPES).transpose(1, 0, 2).reshape(STRIPES, ROWS)
        shuffled = jax.vmap(lambda row_key, row_values: row_values[jax.random.permutation(row_key, ROWS)])(jax.random.split(second_key, STRIPES), by_source)
        return shuffled.reshape(VARIANTS)
    return jax.vmap(one_cohort)(cohort_keys).astype(jnp.int32)


def draw_precision(key, part):
    first_key, second_key = jax.random.split(key)
    position = jnp.arange(COHORTS, dtype=jnp.float32) / max(COHORTS - 1, 1)
    rising = jnp.exp(math.log(3.0) * position)[:, None]
    cohort_size = jnp.exp(jax.random.uniform(first_key, (COHORTS, 1), minval=0.0, maxval=math.log(100.0))) * rising
    quality = jax.random.uniform(second_key, (COHORTS, VARIANTS), minval=0.5, maxval=1.0)
    return (cohort_size * quality).astype(jnp.float32)


def draw_reference_panel(key, part):
    base_key, column_key = jax.random.split(key, 2)
    base = jnp.clip(jax.random.normal(base_key, (N_REF, VARIANTS), jnp.float32), -6.0, 6.0)
    column_scale = jnp.exp(jax.random.uniform(column_key, (1, VARIANTS), minval=math.log(0.2), maxval=math.log(0.7)))
    values = base * column_scale
    return values.astype(jnp.bfloat16)


def gene_windows(key):
    length_key, offset_key = jax.random.split(jax.random.fold_in(key, 17))
    stripe_ids = jnp.arange(STRIPES, dtype=jnp.int32)[:, None]
    gene_ids = jnp.arange(GENES_DEV, dtype=jnp.int32)[None, :]
    spans_len = jax.random.randint(length_key, (STRIPES, GENES_DEV), L_MAX // 8, L_MAX + 1, dtype=jnp.int32)
    leading = gene_ids == 0
    final = stripe_ids == STRIPES - 1
    closing = jnp.logical_and(final, gene_ids == GENES_DEV - 1)
    spans_len = jnp.where(leading, L_MAX, spans_len)
    spans_len = jnp.where(closing, L_MAX // 8, spans_len)
    ranges = jnp.where(final, ROWS - spans_len + 1, ROWS)
    offsets = jax.random.randint(offset_key, (STRIPES, GENES_DEV), 0, ranges, dtype=jnp.int32)
    begins = stripe_ids * ROWS + offsets
    crossing = stripe_ids * ROWS + ROWS - spans_len // 2
    begins = jnp.where(jnp.logical_and(leading, jnp.logical_not(final)), crossing, begins)
    begins = jnp.where(closing, VARIANTS - L_MAX // 8, begins)
    return (begins.reshape(GENES).astype(jnp.int32), spans_len.reshape(GENES).astype(jnp.int32))


def draw_window_start(key, part):
    return gene_windows(key)[0]


def draw_window_length(key, part):
    return gene_windows(key)[1]


def touch_ends(entries, rng, least, top_value):
    shape = entries.shape
    index_at = [jax.random.randint(jax.random.fold_in(rng, axis), (), 0, shape[axis]) for axis in range(len(shape))]
    entries = entries.at[tuple(index_at)].set(least)
    longest = shape.index(max(shape))
    index_at[longest] = (index_at[longest] + 1) % shape[longest]
    return entries.at[tuple(index_at)].set(top_value)


def strengthened(entries, key, source, target, parts, factor):
    owner, partner = [(jnp.arange(entries.shape[dim]) // (entries.shape[dim] // parts)).reshape([-1 if axis == dim else 1 for axis in range(entries.ndim)]) for dim in (source, target)]
    chosen = jax.random.permutation(key, parts)[partner]
    strong = (owner == chosen) | (owner == (partner + parts // 2) % parts)
    return jnp.where(strong, factor * entries, entries)


def steps_of(rng, shape, cuts, least, top_value):
    level = 1.0
    for dim, parts in cuts:
        steps = jax.random.uniform(jax.random.fold_in(jax.random.fold_in(rng, 6), dim), (parts,), jnp.float32, least / len(cuts), top_value / len(cuts))
        level = level * jnp.repeat(jnp.exp(steps), shape[dim] // parts).reshape((-1,) + (1,) * (len(shape) - 1 - dim))
    return level


def scatter_about(stream_key, dims, spread, limit, cuts=(), held_as=jnp.bfloat16):
    values = spread * jax.random.normal(stream_key, dims, jnp.float32)
    if cuts:
        values = values * steps_of(stream_key, dims, cuts, -0.22, 0.18)
    return jnp.clip(values, -limit, limit).astype(held_as)


def noise_with(own_key, dims, scale, bound, cuts, heavy, kind=jnp.bfloat16):
    values = scale * jax.random.normal(own_key, dims, jnp.float32)
    if cuts:
        values = values * steps_of(own_key, dims, cuts, -0.22, 0.18)
    return jnp.clip(strengthened(values, jax.random.fold_in(own_key, 3), *heavy), -bound, bound).astype(kind)


def setup_inputs(seed: int = 0) -> dict:
    splits = jax.random.split(jax.random.key(seed), 9)
    cohort_scores = noise_with(splits[0], (COHORTS, VARIANTS, TRAITS), 1.0, 6.0, ((0, 8), (1, 4)), (0, 2, 8, 2.0))
    allele_match = draw_allele_match(jax.random.fold_in(splits[8], 71), 0)
    allele_flip = touch_ends((jax.random.randint(splits[2], (COHORTS, VARIANTS), 0, 3) < 1).astype(jnp.int32), jax.random.fold_in(splits[2], 1), 0, 1)
    precision = draw_precision(jax.random.fold_in(splits[8], 71), 0)
    reference_panel = draw_reference_panel(jax.random.fold_in(splits[8], 71), 0)
    gene_weights = scatter_about(splits[5], (GENES, TISSUES, L_MAX), L_MAX ** -0.5, 0.09375, ((0, 4),))
    window_start = draw_window_start(jax.random.fold_in(splits[8], 71), 0)
    window_length = draw_window_length(jax.random.fold_in(splits[8], 71), 0)
    return {"cohort_scores": cohort_scores, "allele_match": allele_match, "allele_flip": allele_flip, "precision": precision, "reference_panel": reference_panel, "gene_weights": gene_weights, "window_start": window_start, "window_length": window_length}


EPSILON = 1e-06

def reference(cohort_scores, allele_match, allele_flip, precision, reference_panel, gene_weights, window_start, window_length):

    def add_cohort(running, inputs):
        rows_here, match_here, flip_here, weight_here = inputs
        signs = (1 - 2 * flip_here).astype(jnp.bfloat16)
        flipped = rows_here * signs[:, None]
        aligned = jnp.zeros((VARIANTS, TRAITS), jnp.bfloat16).at[match_here.astype(jnp.int32)].set(flipped)
        weighted = (jnp.sqrt(weight_here)[:, None] * aligned).astype(jnp.bfloat16)
        return (running + weighted.astype(jnp.float32), None)
    summed, _ = lax.scan(add_cohort, jnp.zeros((VARIANTS, TRAITS), jnp.float32), (cohort_scores, allele_match, allele_flip, precision))
    total_weight = lax.optimization_barrier(jnp.sum(precision, axis=0))
    combined = (summed.T / jnp.sqrt(total_weight)[None, :]).astype(jnp.bfloat16)
    panel_ext = jnp.concatenate([reference_panel, jnp.zeros((N_REF, L_MAX), jnp.bfloat16)], axis=1)
    score_ext = jnp.concatenate([combined, jnp.zeros((TRAITS, L_MAX), jnp.bfloat16)], axis=1)

    def one_gene(inputs):
        weight_gene, begin, size = inputs
        keep = jnp.arange(L_MAX) < size
        masked = jnp.where(keep[None, :], weight_gene, jnp.zeros_like(weight_gene))
        columns = lax.dynamic_slice(panel_ext, (jnp.int32(0), begin.astype(jnp.int32)), (N_REF, L_MAX))
        projected = jnp.dot(columns, masked.T, preferred_element_type=jnp.float32)
        variance = lax.optimization_barrier(jnp.sum(projected * projected, axis=0)) / N_REF
        window = lax.dynamic_slice(score_ext, (jnp.int32(0), begin.astype(jnp.int32)), (TRAITS, L_MAX))
        numerator = jnp.dot(masked, window.T, preferred_element_type=jnp.float32)
        return numerator / jnp.sqrt(variance + EPSILON)[:, None]
    return lax.map(one_gene, (gene_weights, window_start, window_length))
```

```python
import functools

import jax
import jax.numpy as jnp
from jax import lax
from jax.experimental import pallas as pl
from jax.experimental.pallas import tpu as pltpu
from jax.sharding import PartitionSpec as P

EPSILON = 1e-06


def passed_along(block, axis, distance):
    devices = range(lax.axis_size(axis))
    route = [(i - distance, i) for i in devices if i - distance in devices]
    return lax.ppermute(block, axis, route)


def general_device(
    cohort_scores,
    allele_match,
    allele_flip,
    precision,
    reference_panel,
    gene_weights,
    window_start,
    window_length,
):
    row_count = cohort_scores.shape[1]
    trait_count = cohort_scores.shape[2]
    stripe_count = lax.axis_size("stripe")
    cohort_count = lax.axis_size("cohort")
    bucket_rows = row_count // stripe_count
    block_traits = trait_count // cohort_count
    person_count = reference_panel.shape[0]
    gene_count = gene_weights.shape[0]
    tissue_count = gene_weights.shape[1]
    window_span = gene_weights.shape[2]
    step_width = min(512, window_span)
    first_variant = lax.axis_index("stripe") * row_count
    target = allele_match[0] // row_count
    inside = allele_match[0] - target * row_count
    member = (target[:, None] == jnp.arange(stripe_count, dtype=jnp.int32)[None, :]).astype(
        jnp.int32
    )
    ranking = jnp.sum(jnp.cumsum(member, axis=0) * member, axis=1) - 1
    placing = target * bucket_rows + ranking
    signs = (1 - 2 * allele_flip[0]).astype(jnp.bfloat16)
    flipped = cohort_scores[0] * signs[:, None]
    outgoing = jnp.zeros((row_count, trait_count), jnp.bfloat16).at[placing].set(flipped)
    out_keys = jnp.zeros((row_count,), jnp.int32).at[placing].set(inside)
    got_rows, got_keys = (
        lax.all_to_all(
            outgoing.reshape(stripe_count, bucket_rows, trait_count),
            "stripe",
            split_axis=0,
            concat_axis=0,
            tiled=True,
        ),
        lax.all_to_all(
            out_keys.reshape(stripe_count, bucket_rows),
            "stripe",
            split_axis=0,
            concat_axis=0,
            tiled=True,
        ),
    )
    aligned = (
        jnp.zeros((row_count, trait_count), jnp.bfloat16)
        .at[got_keys.reshape(row_count)]
        .set(got_rows.reshape(row_count, trait_count))
    )
    own_weight = precision[0]
    weighted = (jnp.sqrt(own_weight)[:, None] * aligned).astype(jnp.bfloat16)
    total_weight = lax.psum(own_weight, "cohort")
    received = lax.all_to_all(weighted, "cohort", split_axis=1, concat_axis=1, tiled=True)
    summed = jnp.sum(
        received.reshape(row_count, cohort_count, block_traits).astype(jnp.float32), axis=1
    )
    combined = (summed.T / jnp.sqrt(total_weight)[None, :]).astype(jnp.bfloat16)
    joined = jnp.concatenate([reference_panel, combined], axis=0)
    moved = passed_along(joined, "stripe", -1)
    panel_rim = moved[:person_count]
    score_rim = moved[person_count:]
    panel_ext = jnp.concatenate([reference_panel, panel_rim], axis=1)
    score_ext = jnp.concatenate([combined, score_rim], axis=1)

    def weight_block(gene, block, size):
        offset = block * step_width
        piece = lax.dynamic_slice(
            gene_weights[gene], (jnp.int32(0), offset), (tissue_count, step_width)
        )
        keep = offset + jnp.arange(step_width, dtype=jnp.int32) < size
        return jnp.where(keep[None, :], piece, jnp.zeros_like(piece))

    def window_variance(gene, size):
        begin = window_start[gene] - first_variant

        def add_block(block, running):
            columns = lax.dynamic_slice(
                panel_ext, (jnp.int32(0), begin + block * step_width), (person_count, step_width)
            )
            piece = weight_block(gene, block, size)
            return running + lax.dot_general(
                columns, piece, (((1,), (1,)), ((), ())), preferred_element_type=jnp.float32
            )

        blocks_needed = (size + step_width - 1) // step_width
        projected = lax.fori_loop(
            0, blocks_needed, add_block, jnp.zeros((person_count, tissue_count), jnp.float32)
        )
        return jnp.sum(projected * projected, axis=0) / person_count

    def window_score(gene):
        begin = window_start[gene] - first_variant
        size = window_length[gene]

        def add_block(block, running):
            window = lax.dynamic_slice(
                score_ext, (jnp.int32(0), begin + block * step_width), (block_traits, step_width)
            )
            piece = weight_block(gene, block, size)
            return running + lax.dot_general(
                piece, window, (((1,), (1,)), ((), ())), preferred_element_type=jnp.float32
            )

        blocks_needed = (size + step_width - 1) // step_width
        return lax.fori_loop(
            0, blocks_needed, add_block, jnp.zeros((tissue_count, block_traits), jnp.float32)
        )

    empty = jnp.zeros((gene_count, tissue_count), jnp.float32)

    def every_gene(gene, partial_value):
        return partial_value.at[gene].set(window_variance(gene, window_length[gene]))

    variance = lax.fori_loop(0, gene_count, every_gene, empty)

    def score_gene(gene, partial_value):
        return partial_value.at[gene].set(window_score(gene))

    numerator = lax.fori_loop(
        0, gene_count, score_gene, jnp.zeros((gene_count, tissue_count, block_traits), jnp.float32)
    )
    return numerator / jnp.sqrt(variance + EPSILON)[:, :, None]


MESH = pl.DeviceIdType.MESH
BF16 = jnp.bfloat16
F32 = jnp.float32
Y_COUNT = 2
CHUNKS = 6


def pack_kernel(low_ref, high_ref, left_ref, slot_ref, out_ref, total):
    block = pl.program_id(0)
    width = out_ref.shape[2]
    depth = left_ref.shape[1] // 4
    total[...] = jnp.zeros_like(total)
    lane = lax.broadcasted_iota(jnp.int32, (depth, 128), 1) + block * width

    def add_rows(k, carry):
        start = pl.multiple_of(k * depth, depth)
        slots = slot_ref[pl.ds(start, depth), :]
        chosen = jnp.concatenate(
            [
                jnp.where(slots == lane + 128 * b, 1.0, 0.0).astype(BF16)
                for b in range(width // 128)
            ],
            axis=1,
        )
        total[...] += jnp.dot(
            left_ref[:, pl.ds(start, depth)], chosen, preferred_element_type=F32
        )
        return carry

    lax.fori_loop(low_ref[block], high_ref[block], add_rows, 0)
    out_ref[0] = total[...].astype(BF16)


def pack_rows(left, slot, low, high, stripes):
    height, rows = left.shape
    bucket = rows // stripes
    width = bucket // 3
    return pl.pallas_call(
        pack_kernel,
        grid_spec=pltpu.PrefetchScalarGridSpec(
            num_scalar_prefetch=2,
            grid=(stripes * 3,),
            in_specs=[
                pl.BlockSpec((height, rows), lambda i, lo, hi: (0, 0)),
                pl.BlockSpec((rows, 128), lambda i, lo, hi: (0, 0)),
            ],
            out_specs=pl.BlockSpec((1, height, width), lambda i, lo, hi: (i // 3, 0, i % 3)),
            scratch_shapes=[pltpu.VMEM((height, width), F32)],
        ),
        out_shape=jax.ShapeDtypeStruct((stripes, height, bucket), BF16),
        cost_estimate=pl.CostEstimate(
            flops=height * rows * rows, bytes_accessed=4 * height * rows, transcendentals=0
        ),
    )(low, high, left, slot)


def combine_kernel(
    z_count,
    got_ref,
    key_ref,
    precision_ref,
    out_ref,
    own,
    y_got,
    pair,
    z_got,
    weights,
    root,
    total,
    y_send,
    y_recv,
    z_send,
    z_recv,
    w_send,
    w_recv,
):
    cohort = lax.axis_index("cohort")
    stripe = lax.axis_index("stripe")
    cohorts = z_count * Y_COUNT
    z, y = cohort // Y_COUNT, lax.rem(cohort, Y_COUNT)
    stripes, traits, bucket = got_ref.shape
    block = traits // cohorts
    width = own.shape[4]

    barrier = pltpu.get_barrier_semaphore()
    for d in range(1, cohorts):
        pl.semaphore_signal(
            barrier, inc=1, device_id=(lax.rem(cohort + d, cohorts), stripe), device_id_type=MESH
        )
    pl.semaphore_wait(barrier, cohorts - 1)

    def weight_copy(d):
        return pltpu.make_async_remote_copy(
            src_ref=precision_ref,
            dst_ref=weights.at[d],
            send_sem=w_send.at[d],
            recv_sem=w_recv.at[d],
            device_id=(lax.rem(cohort + d, cohorts), stripe),
            device_id_type=MESH,
        )

    def y_copy(k):
        return pltpu.make_async_remote_copy(
            src_ref=own.at[k, 1 - y],
            dst_ref=y_got.at[k],
            send_sem=y_send.at[k],
            recv_sem=y_recv.at[k],
            device_id=(z * Y_COUNT + 1 - y, stripe),
            device_id_type=MESH,
        )

    def z_copy(k, d):
        other = lax.rem(z + d, z_count)
        return pltpu.make_async_remote_copy(
            src_ref=pair.at[k, other],
            dst_ref=z_got.at[k, d],
            send_sem=z_send.at[k, d],
            recv_sem=z_recv.at[k, d],
            device_id=(other * Y_COUNT + y, stripe),
            device_id_type=MESH,
        )

    for d in range(1, cohorts):
        weight_copy(d).start()
    root[...] = jnp.sqrt(precision_ref[...])

    def step(k, carry):
        @pl.when(k < CHUNKS)
        def _():
            lane = lax.broadcasted_iota(jnp.int32, (bucket, 128), 1) + k * width
            total[...] = jnp.zeros_like(total)

            def add_source(s, inner):
                keys = key_ref[pl.ds(pl.multiple_of(s * bucket, bucket), bucket), :]
                chosen = jnp.concatenate(
                    [
                        jnp.where(keys == lane + 128 * b, 1.0, 0.0).astype(BF16)
                        for b in range(width // 128)
                    ],
                    axis=1,
                )
                total[...] += jnp.dot(got_ref[s], chosen, preferred_element_type=F32)
                return inner

            lax.fori_loop(0, stripes, add_source, 0)
            scale = root[:, pl.ds(pl.multiple_of(k * width, width), width)]
            for c in range(cohorts):
                own[k, c % Y_COUNT, c // Y_COUNT] = (
                    total[c * block : (c + 1) * block, :] * scale
                ).astype(BF16)
            y_copy(k).start()

        @pl.when(k >= 1)
        def _():
            last = k - 1
            y_copy(last).wait_recv()
            for zi in range(z_count):
                pair[last, zi] = (
                    own[last, y, zi].astype(F32) + y_got[last, zi].astype(F32)
                ).astype(BF16)
            for d in range(1, z_count):
                z_copy(last, d).start()

        return carry

    lax.fori_loop(0, CHUNKS + 1, step, 0)

    weight_sum = precision_ref[...]
    for d in range(1, cohorts):
        weight_copy(d).wait_recv()
        weight_sum = weight_sum + weights[d]
    root[...] = jnp.sqrt(weight_sum)

    def finish(k, carry):
        summed = pair[k, z].astype(F32)
        for d in range(1, z_count):
            z_copy(k, d).wait_recv()
            summed = summed + z_got[k, d].astype(F32)
        here = pl.ds(pl.multiple_of(k * width, width), width)
        out_ref[:, here] = (summed / root[:, here]).astype(BF16)
        y_copy(k).wait_send()
        for d in range(1, z_count):
            z_copy(k, d).wait_send()
        return carry

    lax.fori_loop(0, CHUNKS, finish, 0)
    for d in range(1, cohorts):
        weight_copy(d).wait_send()


def combine(got, keys, precision, cohorts):
    stripes, traits, bucket = got.shape
    rows = stripes * bucket
    width = rows // CHUNKS
    block = traits // cohorts
    z_count = cohorts // Y_COUNT
    vmem = pl.BlockSpec(memory_space=pltpu.VMEM)
    dma = pltpu.SemaphoreType.DMA
    return pl.pallas_call(
        functools.partial(combine_kernel, z_count),
        out_shape=jax.ShapeDtypeStruct((block, rows), BF16),
        in_specs=[vmem] * 3,
        out_specs=vmem,
        scratch_shapes=[
            pltpu.VMEM((CHUNKS, Y_COUNT, z_count, block, width), BF16),
            pltpu.VMEM((CHUNKS, z_count, block, width), BF16),
            pltpu.VMEM((CHUNKS, z_count, block, width), BF16),
            pltpu.VMEM((CHUNKS, z_count, block, width), BF16),
            pltpu.VMEM((cohorts, 1, rows), F32),
            pltpu.VMEM((1, rows), F32),
            pltpu.VMEM((traits, width), F32),
            dma((CHUNKS,)),
            dma((CHUNKS,)),
            dma((CHUNKS, z_count)),
            dma((CHUNKS, z_count)),
            dma((cohorts,)),
            dma((cohorts,)),
        ],
        compiler_params=pltpu.CompilerParams(collective_id=0, has_side_effects=True),
    )(got, keys, precision)


def window_product(begin, size, weight_ref, side_ref, total):
    span = weight_ref.shape[2]
    step = span // 4
    blocks = step // 128
    shift = lax.rem(begin, 128)
    base = begin - shift
    lane = lax.broadcasted_iota(jnp.int32, (weight_ref.shape[1], 128), 1)
    total[...] = jnp.zeros_like(total)

    def add_part(part, carry):
        first = part * blocks

        def turned(b):
            at = jnp.clip(first + b, 0, span // 128 - 1)
            piece = weight_ref[0, :, pl.ds(pl.multiple_of(at * 128, 128), 128)]
            return pltpu.roll(piece.astype(F32), shift, 1)

        before = turned(-1)
        made = []
        for b in range(blocks):
            after = turned(b)
            place = (first + b) * 128 + lane - shift
            keep = jnp.logical_and(place >= 0, place < size)
            made.append(
                jnp.where(keep, jnp.where(lane < shift, before, after), 0.0).astype(BF16)
            )
            before = after
        columns = side_ref[:, pl.ds(pl.multiple_of(base + first * 128, 128), step)]
        total[...] += lax.dot_general(
            jnp.concatenate(made, axis=1),
            columns,
            (((1,), (1,)), ((), ())),
            preferred_element_type=F32,
        )
        return carry

    lax.fori_loop(0, (size + shift + step - 1) // step, add_part, 0)


def variance_kernel(begin_ref, size_ref, weight_ref, side_ref, out_ref, total):
    gene = pl.program_id(0)
    window_product(begin_ref[gene], size_ref[gene], weight_ref, side_ref, total)
    projected = total[...]
    out_ref[0] = jnp.sum(projected * projected, axis=1, keepdims=True)


def score_kernel(begin_ref, size_ref, weight_ref, side_ref, variance_ref, out_ref, total):
    gene = pl.program_id(0)
    window_product(begin_ref[gene], size_ref[gene], weight_ref, side_ref, total)
    out_ref[0] = total[...] / jnp.sqrt(variance_ref[0] + EPSILON)


def by_gene(kernel, begin, size, weights, side, extra, width):
    genes, tissues, span = weights.shape
    column = pl.BlockSpec((1, tissues, 1), lambda g, b, s: (g, 0, 0))
    return pl.pallas_call(
        kernel,
        grid_spec=pltpu.PrefetchScalarGridSpec(
            num_scalar_prefetch=2,
            grid=(genes,),
            in_specs=[
                pl.BlockSpec((1, tissues, span), lambda g, b, s: (g, 0, 0)),
                pl.BlockSpec(side.shape, lambda g, b, s: (0, 0)),
            ]
            + [column] * len(extra),
            out_specs=pl.BlockSpec((1, tissues, width), lambda g, b, s: (g, 0, 0)),
            scratch_shapes=[pltpu.VMEM((tissues, side.shape[0]), F32)],
        ),
        out_shape=jax.ShapeDtypeStruct((genes, tissues, width), F32),
        cost_estimate=pl.CostEstimate(
            flops=2 * genes * tissues * span * side.shape[0],
            bytes_accessed=2 * genes * tissues * span,
            transcendentals=0,
        ),
    )(begin, size, weights, side, *extra)


def extended(block, step):
    rim = passed_along(block, "stripe", -1)
    return jnp.concatenate([block, rim, jnp.zeros((block.shape[0], step), BF16)], axis=1)


def fast_device(
    cohort_scores,
    allele_match,
    allele_flip,
    precision,
    reference_panel,
    gene_weights,
    window_start,
    window_length,
):
    row_count, trait_count = cohort_scores.shape[1:]
    stripes = lax.axis_size("stripe")
    cohorts = lax.axis_size("cohort")
    bucket = row_count // stripes
    persons = reference_panel.shape[0]
    step = gene_weights.shape[2] // 4
    begin = window_start - lax.axis_index("stripe") * row_count

    share = persons // cohorts
    panel = lax.dynamic_slice_in_dim(
        reference_panel, lax.axis_index("cohort") * share, share, axis=0
    )
    panel_ext = extended(panel, step)

    match = allele_match[0]
    target = match // row_count
    inside = match - target * row_count
    member = target[None, :] == jnp.arange(stripes, dtype=jnp.int32)[:, None]
    ranking = jnp.cumsum(member.astype(jnp.int32), axis=1)
    rank = jnp.sum(jnp.where(member, ranking, 0), axis=0) - 1
    slot = target * bucket + rank
    width = bucket // 3
    depth = row_count // 4
    ends = ranking[:, depth - 1 :: depth]
    edges = jnp.arange(3, dtype=jnp.int32) * width
    low = jnp.sum(ends[:, None, :] <= edges[None, :, None], axis=2, dtype=jnp.int32)
    high = 1 + jnp.sum(ends[:, None, :] < (edges + width)[None, :, None], axis=2, dtype=jnp.int32)
    signs = (1 - 2 * allele_flip[0]).astype(BF16)
    left = jnp.concatenate(
        [
            (cohort_scores[0] * signs[:, None]).T,
            (inside // 64).astype(BF16)[None, :],
            lax.rem(inside, 64).astype(BF16)[None, :],
            jnp.zeros((14, row_count), BF16),
        ],
        axis=0,
    )
    outgoing = pack_rows(
        left,
        jnp.broadcast_to(slot[:, None], (row_count, 128)),
        low.reshape(-1),
        high.reshape(-1),
        stripes,
    )
    got = lax.all_to_all(outgoing, "stripe", split_axis=0, concat_axis=0, tiled=True)

    squares = by_gene(variance_kernel, begin, window_length, gene_weights, panel_ext, (), 1)
    shares = lax.all_to_all(
        jnp.broadcast_to(squares[:, :, 0][None], (cohorts,) + squares.shape[:2]),
        "cohort",
        split_axis=0,
        concat_axis=0,
        tiled=True,
    )
    variance = jnp.sum(shares, axis=0)[:, :, None] / persons

    keys = (
        64 * got[:, trait_count].astype(jnp.int32) + got[:, trait_count + 1].astype(jnp.int32)
    ).reshape(row_count)
    combined = combine(
        got[:, :trait_count],
        jnp.broadcast_to(keys[:, None], (row_count, 128)),
        precision,
        cohorts,
    )
    score_ext = extended(combined, step)
    return by_gene(
        score_kernel,
        begin,
        window_length,
        gene_weights,
        score_ext,
        (variance,),
        combined.shape[0],
    )


def on_device(cohort_scores, *others):
    rows, traits = cohort_scores.shape[1:]
    stripes = lax.axis_size("stripe")
    cohorts = lax.axis_size("cohort")
    span = others[4].shape[2]
    fits = (
        cohorts % Y_COUNT == 0
        and traits % (16 * cohorts) == 0
        and rows % (384 * stripes) == 0
        and rows % (128 * CHUNKS) == 0
        and rows < 16384
        and span % 512 == 0
        and span <= rows
        and others[3].shape[0] % (16 * cohorts) == 0
    )
    if fits:
        return fast_device(cohort_scores, *others)
    return general_device(cohort_scores, *others)


def solution(mesh):
    in_specs = (
        P("cohort", "stripe", None),
        P("cohort", "stripe"),
        P("cohort", "stripe"),
        P("cohort", "stripe"),
        P(None, "stripe"),
        P("stripe", None, None),
        P("stripe"),
        P("stripe"),
    )
    out_specs = P("stripe", None, "cohort")
    return jax.shard_map(
        on_device, mesh=mesh, in_specs=in_specs, out_specs=out_specs, check_vma=False
    )
```

```python
import functools

import jax
import jax.numpy as jnp
from jax import lax
from jax.experimental import pallas as pl
from jax.experimental.pallas import tpu as pltpu
from jax.sharding import PartitionSpec as P

EPSILON = 1e-06


def passed_along(block, axis, distance):
    devices = range(lax.axis_size(axis))
    route = [(i - distance, i) for i in devices if i - distance in devices]
    return lax.ppermute(block, axis, route)


def general_device(
    cohort_scores,
    allele_match,
    allele_flip,
    precision,
    reference_panel,
    gene_weights,
    window_start,
    window_length,
):
    row_count = cohort_scores.shape[1]
    trait_count = cohort_scores.shape[2]
    stripe_count = lax.axis_size("stripe")
    cohort_count = lax.axis_size("cohort")
    bucket_rows = row_count // stripe_count
    block_traits = trait_count // cohort_count
    person_count = reference_panel.shape[0]
    gene_count = gene_weights.shape[0]
    tissue_count = gene_weights.shape[1]
    window_span = gene_weights.shape[2]
    step_width = min(512, window_span)
    first_variant = lax.axis_index("stripe") * row_count
    target = allele_match[0] // row_count
    inside = allele_match[0] - target * row_count
    member = (target[:, None] == jnp.arange(stripe_count, dtype=jnp.int32)[None, :]).astype(
        jnp.int32
    )
    ranking = jnp.sum(jnp.cumsum(member, axis=0) * member, axis=1) - 1
    placing = target * bucket_rows + ranking
    signs = (1 - 2 * allele_flip[0]).astype(jnp.bfloat16)
    flipped = cohort_scores[0] * signs[:, None]
    outgoing = jnp.zeros((row_count, trait_count), jnp.bfloat16).at[placing].set(flipped)
    out_keys = jnp.zeros((row_count,), jnp.int32).at[placing].set(inside)
    got_rows, got_keys = (
        lax.all_to_all(
            outgoing.reshape(stripe_count, bucket_rows, trait_count),
            "stripe",
            split_axis=0,
            concat_axis=0,
            tiled=True,
        ),
        lax.all_to_all(
            out_keys.reshape(stripe_count, bucket_rows),
            "stripe",
            split_axis=0,
            concat_axis=0,
            tiled=True,
        ),
    )
    aligned = (
        jnp.zeros((row_count, trait_count), jnp.bfloat16)
        .at[got_keys.reshape(row_count)]
        .set(got_rows.reshape(row_count, trait_count))
    )
    own_weight = precision[0]
    weighted = (jnp.sqrt(own_weight)[:, None] * aligned).astype(jnp.bfloat16)
    total_weight = lax.psum(own_weight, "cohort")
    received = lax.all_to_all(weighted, "cohort", split_axis=1, concat_axis=1, tiled=True)
    summed = jnp.sum(
        received.reshape(row_count, cohort_count, block_traits).astype(jnp.float32), axis=1
    )
    combined = (summed.T / jnp.sqrt(total_weight)[None, :]).astype(jnp.bfloat16)
    joined = jnp.concatenate([reference_panel, combined], axis=0)
    moved = passed_along(joined, "stripe", -1)
    panel_rim = moved[:person_count]
    score_rim = moved[person_count:]
    panel_ext = jnp.concatenate([reference_panel, panel_rim], axis=1)
    score_ext = jnp.concatenate([combined, score_rim], axis=1)

    def weight_block(gene, block, size):
        offset = block * step_width
        piece = lax.dynamic_slice(
            gene_weights[gene], (jnp.int32(0), offset), (tissue_count, step_width)
        )
        keep = offset + jnp.arange(step_width, dtype=jnp.int32) < size
        return jnp.where(keep[None, :], piece, jnp.zeros_like(piece))

    def window_variance(gene, size):
        begin = window_start[gene] - first_variant

        def add_block(block, running):
            columns = lax.dynamic_slice(
                panel_ext, (jnp.int32(0), begin + block * step_width), (person_count, step_width)
            )
            piece = weight_block(gene, block, size)
            return running + lax.dot_general(
                columns, piece, (((1,), (1,)), ((), ())), preferred_element_type=jnp.float32
            )

        blocks_needed = (size + step_width - 1) // step_width
        projected = lax.fori_loop(
            0, blocks_needed, add_block, jnp.zeros((person_count, tissue_count), jnp.float32)
        )
        return jnp.sum(projected * projected, axis=0) / person_count

    def window_score(gene):
        begin = window_start[gene] - first_variant
        size = window_length[gene]

        def add_block(block, running):
            window = lax.dynamic_slice(
                score_ext, (jnp.int32(0), begin + block * step_width), (block_traits, step_width)
            )
            piece = weight_block(gene, block, size)
            return running + lax.dot_general(
                piece, window, (((1,), (1,)), ((), ())), preferred_element_type=jnp.float32
            )

        blocks_needed = (size + step_width - 1) // step_width
        return lax.fori_loop(
            0, blocks_needed, add_block, jnp.zeros((tissue_count, block_traits), jnp.float32)
        )

    empty = jnp.zeros((gene_count, tissue_count), jnp.float32)

    def every_gene(gene, partial_value):
        return partial_value.at[gene].set(window_variance(gene, window_length[gene]))

    variance = lax.fori_loop(0, gene_count, every_gene, empty)

    def score_gene(gene, partial_value):
        return partial_value.at[gene].set(window_score(gene))

    numerator = lax.fori_loop(
        0, gene_count, score_gene, jnp.zeros((gene_count, tissue_count, block_traits), jnp.float32)
    )
    return numerator / jnp.sqrt(variance + EPSILON)[:, :, None]


MESH = pl.DeviceIdType.MESH
BF16 = jnp.bfloat16
F32 = jnp.float32
Y_COUNT = 2
CHUNKS = 6


def spread_column(row):
    return jnp.transpose(jnp.broadcast_to(row, (128, 128)))


def pack_kernel(low_ref, high_ref, left_ref, slot_ref, out_ref, total, column):
    block = pl.program_id(0)
    width = out_ref.shape[2]
    depth = left_ref.shape[1] // 4
    total[...] = jnp.zeros_like(total)
    lane = (lax.broadcasted_iota(jnp.int32, (depth, 128), 1) + block * width).astype(F32)

    @pl.when(block == 0)
    def _():
        for b in range(slot_ref.shape[0]):
            column[b * 128 : (b + 1) * 128, :] = spread_column(slot_ref[b : b + 1, :])

    def add_rows(k, carry):
        start = pl.multiple_of(k * depth, depth)
        slots = column[pl.ds(start, depth), :]
        chosen = jnp.concatenate(
            [
                jnp.where(slots == lane + 128 * b, 1.0, 0.0).astype(BF16)
                for b in range(width // 128)
            ],
            axis=1,
        )
        total[...] += jnp.dot(
            left_ref[:, pl.ds(start, depth)], chosen, preferred_element_type=F32
        )
        return carry

    lax.fori_loop(low_ref[block], high_ref[block], add_rows, 0)
    out_ref[0] = total[...].astype(BF16)


def pack_rows(left, slot, low, high, stripes):
    height, rows = left.shape
    bucket = rows // stripes
    width = bucket // 3
    return pl.pallas_call(
        pack_kernel,
        grid_spec=pltpu.PrefetchScalarGridSpec(
            num_scalar_prefetch=2,
            grid=(stripes * 3,),
            in_specs=[
                pl.BlockSpec((height, rows), lambda i, lo, hi: (0, 0)),
                pl.BlockSpec(slot.shape, lambda i, lo, hi: (0, 0)),
            ],
            out_specs=pl.BlockSpec((1, height, width), lambda i, lo, hi: (i // 3, 0, i % 3)),
            scratch_shapes=[pltpu.VMEM((height, width), F32), pltpu.VMEM((rows, 128), F32)],
        ),
        out_shape=jax.ShapeDtypeStruct((stripes, height, bucket), BF16),
        cost_estimate=pl.CostEstimate(
            flops=height * rows * rows, bytes_accessed=4 * height * rows, transcendentals=0
        ),
    )(low, high, left, slot)


def combine_kernel(
    z_count,
    traits,
    got_ref,
    precision_ref,
    square_ref,
    out_ref,
    variance_ref,
    column,
    mine,
    rim,
    squares,
    own,
    y_got,
    pair,
    z_got,
    weights,
    root,
    total,
    y_send,
    y_recv,
    z_send,
    z_recv,
    w_send,
    w_recv,
    s_send,
    s_recv,
    r_send,
    r_recv,
):
    cohort = lax.axis_index("cohort")
    stripe = lax.axis_index("stripe")
    cohorts = z_count * Y_COUNT
    z, y = cohort // Y_COUNT, lax.rem(cohort, Y_COUNT)
    stripes, _, bucket = got_ref.shape
    rows = stripes * bucket
    ahead, behind = lax.rem(stripe + 1, stripes), lax.rem(stripe + stripes - 1, stripes)
    block = traits // cohorts
    width = own.shape[4]

    barrier = pltpu.get_barrier_semaphore()
    for d in range(1, cohorts):
        pl.semaphore_signal(
            barrier, inc=1, device_id=(lax.rem(cohort + d, cohorts), stripe), device_id_type=MESH
        )
    for other in (ahead, behind):
        pl.semaphore_signal(barrier, inc=1, device_id=(cohort, other), device_id_type=MESH)
    pl.semaphore_wait(barrier, cohorts + 1)

    def weight_copy(d):
        return pltpu.make_async_remote_copy(
            src_ref=precision_ref,
            dst_ref=weights.at[d],
            send_sem=w_send.at[d],
            recv_sem=w_recv.at[d],
            device_id=(lax.rem(cohort + d, cohorts), stripe),
            device_id_type=MESH,
        )

    def square_copy(d):
        return pltpu.make_async_remote_copy(
            src_ref=square_ref,
            dst_ref=squares.at[d],
            send_sem=s_send.at[d],
            recv_sem=s_recv.at[d],
            device_id=(lax.rem(cohort + d, cohorts), stripe),
            device_id_type=MESH,
        )

    def rim_copy(k):
        return pltpu.make_async_remote_copy(
            src_ref=mine.at[k],
            dst_ref=rim.at[k],
            send_sem=r_send.at[k],
            recv_sem=r_recv.at[k],
            device_id=(cohort, behind),
            device_id_type=MESH,
        )

    def y_copy(k):
        return pltpu.make_async_remote_copy(
            src_ref=own.at[k, 1 - y],
            dst_ref=y_got.at[k],
            send_sem=y_send.at[k],
            recv_sem=y_recv.at[k],
            device_id=(z * Y_COUNT + 1 - y, stripe),
            device_id_type=MESH,
        )

    def z_copy(k, d):
        other = lax.rem(z + d, z_count)
        return pltpu.make_async_remote_copy(
            src_ref=pair.at[k, other],
            dst_ref=z_got.at[k, d],
            send_sem=z_send.at[k, d],
            recv_sem=z_recv.at[k, d],
            device_id=(other * Y_COUNT + y, stripe),
            device_id_type=MESH,
        )

    for d in range(1, cohorts):
        weight_copy(d).start()
        square_copy(d).start()
    root[...] = jnp.sqrt(precision_ref[...])
    out_ref[:, 2 * rows :] = jnp.zeros((block, out_ref.shape[1] - 2 * rows), BF16)

    def spread_keys(s, carry):
        digits = got_ref[s, traits : traits + 16, :].astype(F32)
        keys = 64.0 * digits[0:1] + digits[1:2]
        for b in range(bucket // 128):
            column[pl.ds(pl.multiple_of(s * bucket + b * 128, 128), 128), :] = spread_column(
                keys[:, b * 128 : (b + 1) * 128]
            )
        return carry

    lax.fori_loop(0, stripes, spread_keys, 0)

    def step(k, carry):
        @pl.when(k < CHUNKS)
        def _():
            lane = (lax.broadcasted_iota(jnp.int32, (bucket, 128), 1) + k * width).astype(F32)
            total[...] = jnp.zeros_like(total)

            def add_source(s, inner):
                keys = column[pl.ds(pl.multiple_of(s * bucket, bucket), bucket), :]
                chosen = jnp.concatenate(
                    [
                        jnp.where(keys == lane + 128 * b, 1.0, 0.0).astype(BF16)
                        for b in range(width // 128)
                    ],
                    axis=1,
                )
                total[...] += jnp.dot(got_ref[s, :traits, :], chosen, preferred_element_type=F32)
                return inner

            lax.fori_loop(0, stripes, add_source, 0)
            scale = root[:, pl.ds(pl.multiple_of(k * width, width), width)]
            for c in range(cohorts):
                own[k, c % Y_COUNT, c // Y_COUNT] = (
                    total[c * block : (c + 1) * block, :] * scale
                ).astype(BF16)
            y_copy(k).start()

        @pl.when(k >= 1)
        def _():
            last = k - 1
            y_copy(last).wait_recv()
            for zi in range(z_count):
                pair[last, zi] = (
                    own[last, y, zi].astype(F32) + y_got[last, zi].astype(F32)
                ).astype(BF16)
            for d in range(1, z_count):
                z_copy(last, d).start()

        return carry

    lax.fori_loop(0, CHUNKS + 1, step, 0)

    weight_sum = precision_ref[...]
    for d in range(1, cohorts):
        weight_copy(d).wait_recv()
        weight_sum = weight_sum + weights[d]
    root[...] = jnp.sqrt(weight_sum)

    def finish(k, carry):
        summed = pair[k, z].astype(F32)
        for d in range(1, z_count):
            z_copy(k, d).wait_recv()
            summed = summed + z_got[k, d].astype(F32)
        here = pl.ds(pl.multiple_of(k * width, width), width)
        value = (summed / root[:, here]).astype(BF16)
        mine[k] = value
        out_ref[:, here] = value
        rim_copy(k).start()
        y_copy(k).wait_send()
        for d in range(1, z_count):
            z_copy(k, d).wait_send()
        return carry

    lax.fori_loop(0, CHUNKS, finish, 0)
    square_sum = square_ref[...]
    for d in range(1, cohorts):
        square_copy(d).wait_recv()
        square_sum = square_sum + squares[d]
    variance_ref[...] = square_sum

    def take_rim(k, carry):
        rim_copy(k).wait_recv()
        out_ref[:, pl.ds(pl.multiple_of(rows + k * width, width), width)] = rim[k]
        rim_copy(k).wait_send()
        return carry

    lax.fori_loop(0, CHUNKS, take_rim, 0)
    for d in range(1, cohorts):
        weight_copy(d).wait_send()
        square_copy(d).wait_send()


def combine(got, precision, squares, traits, cohorts, step):
    stripes, _, bucket = got.shape
    rows = stripes * bucket
    width = rows // CHUNKS
    block = traits // cohorts
    z_count = cohorts // Y_COUNT
    vmem = pl.BlockSpec(memory_space=pltpu.VMEM)
    dma = pltpu.SemaphoreType.DMA
    return pl.pallas_call(
        functools.partial(combine_kernel, z_count, traits),
        out_shape=[
            jax.ShapeDtypeStruct((block, 2 * rows + step), BF16),
            jax.ShapeDtypeStruct(squares.shape, F32),
        ],
        in_specs=[vmem] * 3,
        out_specs=[vmem] * 2,
        scratch_shapes=[
            pltpu.VMEM((rows, 128), F32),
            pltpu.VMEM((CHUNKS, block, width), BF16),
            pltpu.VMEM((CHUNKS, block, width), BF16),
            pltpu.VMEM((cohorts,) + squares.shape, F32),
            pltpu.VMEM((CHUNKS, Y_COUNT, z_count, block, width), BF16),
            pltpu.VMEM((CHUNKS, z_count, block, width), BF16),
            pltpu.VMEM((CHUNKS, z_count, block, width), BF16),
            pltpu.VMEM((CHUNKS, z_count, block, width), BF16),
            pltpu.VMEM((cohorts, 1, rows), F32),
            pltpu.VMEM((1, rows), F32),
            pltpu.VMEM((traits, width), F32),
            dma((CHUNKS,)),
            dma((CHUNKS,)),
            dma((CHUNKS, z_count)),
            dma((CHUNKS, z_count)),
            dma((cohorts,)),
            dma((cohorts,)),
            dma((cohorts,)),
            dma((cohorts,)),
            dma((CHUNKS,)),
            dma((CHUNKS,)),
        ],
        compiler_params=pltpu.CompilerParams(collective_id=0, has_side_effects=True),
    )(got, precision, squares)


def variance_kernel(begin_ref, size_ref, weight_ref, side_ref, square_ref, aligned_ref, total):
    group, tissues, span = weight_ref.shape
    step = span // 4
    blocks = step // 128
    lane = lax.broadcasted_iota(jnp.int32, (tissues, 128), 1)

    def one_gene(g, carry):
        gene = pl.program_id(0) * group + g
        size = size_ref[gene]
        shift = lax.rem(begin_ref[gene], 128)
        base = begin_ref[gene] - shift
        total[...] = jnp.zeros_like(total)

        def add_part(part, inner):
            first = part * blocks

            def turned(b):
                at = jnp.clip(first + b, 0, span // 128 - 1)
                piece = weight_ref[g, :, pl.ds(pl.multiple_of(at * 128, 128), 128)]
                return pltpu.roll(piece.astype(F32), shift, 1)

            before = turned(-1)
            made = []
            for b in range(blocks):
                after = turned(b)
                place = (first + b) * 128 + lane - shift
                keep = jnp.logical_and(place >= 0, place < size)
                made.append(
                    jnp.where(keep, jnp.where(lane < shift, before, after), 0.0).astype(BF16)
                )
                before = after
            made = jnp.concatenate(made, axis=1)
            aligned_ref[g, :, pl.ds(pl.multiple_of(first * 128, 128), step)] = made
            columns = side_ref[:, pl.ds(pl.multiple_of(base + first * 128, 128), step)]
            total[...] += lax.dot_general(
                columns, made, (((1,), (1,)), ((), ())), preferred_element_type=F32
            )
            return inner

        lax.fori_loop(0, (size + shift + step - 1) // step, add_part, 0)
        projected = total[...]
        square_ref[g] = jnp.sum(projected * projected, axis=0, keepdims=True)
        return carry

    lax.fori_loop(0, group, one_gene, 0)


def score_kernel(persons, begin_ref, size_ref, aligned_ref, side_ref, square_ref, out_ref, total):
    group, tissues, span = aligned_ref.shape
    step = span // 5

    def one_gene(g, carry):
        gene = pl.program_id(0) * group + g
        shift = lax.rem(begin_ref[gene], 128)
        base = begin_ref[gene] - shift
        total[...] = jnp.zeros_like(total)

        def add_part(part, inner):
            first = part * step
            total[...] += lax.dot_general(
                side_ref[:, pl.ds(pl.multiple_of(base + first, 128), step)],
                aligned_ref[g, :, pl.ds(pl.multiple_of(first, 128), step)],
                (((1,), (1,)), ((), ())),
                preferred_element_type=F32,
            )
            return inner

        lax.fori_loop(0, (size_ref[gene] + shift + step - 1) // step, add_part, 0)
        out_ref[g] = total[...] / jnp.sqrt(square_ref[g] / persons + EPSILON)
        return carry

    lax.fori_loop(0, group, one_gene, 0)


def by_gene(kernel, begin, size, weights, side, extra, outs, group):
    genes, tissues, span = weights.shape

    def rows_of(shape):
        return pl.BlockSpec((group,) + shape[1:], lambda g, b, s: (g, 0, 0))

    return pl.pallas_call(
        kernel,
        grid_spec=pltpu.PrefetchScalarGridSpec(
            num_scalar_prefetch=2,
            grid=(genes // group,),
            in_specs=[
                rows_of(weights.shape),
                pl.BlockSpec(side.shape, lambda g, b, s: (0, 0)),
            ]
            + [rows_of(e.shape) for e in extra],
            out_specs=[rows_of(o.shape) for o in outs],
            scratch_shapes=[pltpu.VMEM((side.shape[0], tissues), F32)],
        ),
        out_shape=outs,
        cost_estimate=pl.CostEstimate(
            flops=16 * genes * tissues * span * side.shape[0],
            bytes_accessed=4 * genes * tissues * span,
            transcendentals=0,
        ),
    )(begin, size, weights, side, *extra)


def extended(block, step):
    rim = passed_along(block, "stripe", -1)
    return jnp.concatenate([block, rim, jnp.zeros((block.shape[0], step), BF16)], axis=1)


def fast_device(
    cohort_scores,
    allele_match,
    allele_flip,
    precision,
    reference_panel,
    gene_weights,
    window_start,
    window_length,
):
    row_count, trait_count = cohort_scores.shape[1:]
    stripes = lax.axis_size("stripe")
    cohorts = lax.axis_size("cohort")
    bucket = row_count // stripes
    persons = reference_panel.shape[0]
    step = gene_weights.shape[2] // 4
    begin = window_start - lax.axis_index("stripe") * row_count

    share = persons // cohorts
    panel = lax.dynamic_slice_in_dim(
        reference_panel, lax.axis_index("cohort") * share, share, axis=0
    )
    panel_ext = extended(panel, step)

    match = allele_match[0]
    target = match // row_count
    inside = match - target * row_count
    member = target[None, :] == jnp.arange(stripes, dtype=jnp.int32)[:, None]
    ranking = jnp.cumsum(member.astype(jnp.int32), axis=1)
    rank = jnp.sum(jnp.where(member, ranking, 0), axis=0) - 1
    slot = target * bucket + rank
    width = bucket // 3
    depth = row_count // 4
    ends = ranking[:, depth - 1 :: depth]
    edges = jnp.arange(3, dtype=jnp.int32) * width
    low = jnp.sum(ends[:, None, :] <= edges[None, :, None], axis=2, dtype=jnp.int32)
    high = 1 + jnp.sum(ends[:, None, :] < (edges + width)[None, :, None], axis=2, dtype=jnp.int32)
    signs = (1 - 2 * allele_flip[0]).astype(BF16)
    left = jnp.concatenate(
        [
            (cohort_scores[0] * signs[:, None]).T,
            (inside // 64).astype(BF16)[None, :],
            lax.rem(inside, 64).astype(BF16)[None, :],
            jnp.zeros((14, row_count), BF16),
        ],
        axis=0,
    )
    outgoing = pack_rows(
        left,
        slot.reshape(row_count // 128, 128).astype(F32),
        low.reshape(-1),
        high.reshape(-1),
        stripes,
    )
    got = lax.all_to_all(outgoing, "stripe", split_axis=0, concat_axis=0, tiled=True)

    genes, tissues, _ = gene_weights.shape
    group = 4 if genes % 4 == 0 else 1
    squares, aligned = by_gene(
        variance_kernel,
        begin,
        window_length,
        gene_weights,
        panel_ext,
        (),
        [
            jax.ShapeDtypeStruct((genes, 1, tissues), F32),
            jax.ShapeDtypeStruct((genes, tissues, 5 * step), BF16),
        ],
        group,
    )
    score_ext, square_sums = combine(got, precision, squares, trait_count, cohorts, step)
    (association,) = by_gene(
        functools.partial(score_kernel, persons),
        begin,
        window_length,
        aligned,
        score_ext,
        (square_sums,),
        [jax.ShapeDtypeStruct((genes, score_ext.shape[0], tissues), F32)],
        group,
    )
    return jnp.transpose(association, (0, 2, 1))


def on_device(cohort_scores, *others):
    rows, traits = cohort_scores.shape[1:]
    stripes = lax.axis_size("stripe")
    cohorts = lax.axis_size("cohort")
    span = others[4].shape[2]
    fits = (
        cohorts % Y_COUNT == 0
        and traits % (16 * cohorts) == 0
        and rows % (384 * stripes) == 0
        and rows % (128 * CHUNKS) == 0
        and rows < 16384
        and span % 512 == 0
        and span <= rows
        and others[3].shape[0] % (16 * cohorts) == 0
    )
    if fits:
        return fast_device(cohort_scores, *others)
    return general_device(cohort_scores, *others)


def solution(mesh):
    in_specs = (
        P("cohort", "stripe", None),
        P("cohort", "stripe"),
        P("cohort", "stripe"),
        P("cohort", "stripe"),
        P(None, "stripe"),
        P("stripe", None, None),
        P("stripe"),
        P("stripe"),
    )
    out_specs = P("stripe", None, "cohort")
    return jax.shard_map(
        on_device, mesh=mesh, in_specs=in_specs, out_specs=out_specs, check_vma=False
    )
```

```python
import functools

import jax
import jax.numpy as jnp
from jax import lax
from jax.experimental import pallas as pl
from jax.experimental.pallas import tpu as pltpu
from jax.sharding import PartitionSpec as P

EPSILON = 1e-06


def passed_along(block, axis, distance):
    devices = range(lax.axis_size(axis))
    route = [(i - distance, i) for i in devices if i - distance in devices]
    return lax.ppermute(block, axis, route)


def general_device(
    cohort_scores,
    allele_match,
    allele_flip,
    precision,
    reference_panel,
    gene_weights,
    window_start,
    window_length,
):
    row_count = cohort_scores.shape[1]
    trait_count = cohort_scores.shape[2]
    stripe_count = lax.axis_size("stripe")
    cohort_count = lax.axis_size("cohort")
    bucket_rows = row_count // stripe_count
    block_traits = trait_count // cohort_count
    person_count = reference_panel.shape[0]
    gene_count = gene_weights.shape[0]
    tissue_count = gene_weights.shape[1]
    window_span = gene_weights.shape[2]
    step_width = min(512, window_span)
    first_variant = lax.axis_index("stripe") * row_count
    target = allele_match[0] // row_count
    inside = allele_match[0] - target * row_count
    member = (target[:, None] == jnp.arange(stripe_count, dtype=jnp.int32)[None, :]).astype(
        jnp.int32
    )
    ranking = jnp.sum(jnp.cumsum(member, axis=0) * member, axis=1) - 1
    placing = target * bucket_rows + ranking
    signs = (1 - 2 * allele_flip[0]).astype(jnp.bfloat16)
    flipped = cohort_scores[0] * signs[:, None]
    outgoing = jnp.zeros((row_count, trait_count), jnp.bfloat16).at[placing].set(flipped)
    out_keys = jnp.zeros((row_count,), jnp.int32).at[placing].set(inside)
    got_rows, got_keys = (
        lax.all_to_all(
            outgoing.reshape(stripe_count, bucket_rows, trait_count),
            "stripe",
            split_axis=0,
            concat_axis=0,
            tiled=True,
        ),
        lax.all_to_all(
            out_keys.reshape(stripe_count, bucket_rows),
            "stripe",
            split_axis=0,
            concat_axis=0,
            tiled=True,
        ),
    )
    aligned = (
        jnp.zeros((row_count, trait_count), jnp.bfloat16)
        .at[got_keys.reshape(row_count)]
        .set(got_rows.reshape(row_count, trait_count))
    )
    own_weight = precision[0]
    weighted = (jnp.sqrt(own_weight)[:, None] * aligned).astype(jnp.bfloat16)
    total_weight = lax.psum(own_weight, "cohort")
    received = lax.all_to_all(weighted, "cohort", split_axis=1, concat_axis=1, tiled=True)
    summed = jnp.sum(
        received.reshape(row_count, cohort_count, block_traits).astype(jnp.float32), axis=1
    )
    combined = (summed.T / jnp.sqrt(total_weight)[None, :]).astype(jnp.bfloat16)
    joined = jnp.concatenate([reference_panel, combined], axis=0)
    moved = passed_along(joined, "stripe", -1)
    panel_rim = moved[:person_count]
    score_rim = moved[person_count:]
    panel_ext = jnp.concatenate([reference_panel, panel_rim], axis=1)
    score_ext = jnp.concatenate([combined, score_rim], axis=1)

    def weight_block(gene, block, size):
        offset = block * step_width
        piece = lax.dynamic_slice(
            gene_weights[gene], (jnp.int32(0), offset), (tissue_count, step_width)
        )
        keep = offset + jnp.arange(step_width, dtype=jnp.int32) < size
        return jnp.where(keep[None, :], piece, jnp.zeros_like(piece))

    def window_variance(gene, size):
        begin = window_start[gene] - first_variant

        def add_block(block, running):
            columns = lax.dynamic_slice(
                panel_ext, (jnp.int32(0), begin + block * step_width), (person_count, step_width)
            )
            piece = weight_block(gene, block, size)
            return running + lax.dot_general(
                columns, piece, (((1,), (1,)), ((), ())), preferred_element_type=jnp.float32
            )

        blocks_needed = (size + step_width - 1) // step_width
        projected = lax.fori_loop(
            0, blocks_needed, add_block, jnp.zeros((person_count, tissue_count), jnp.float32)
        )
        return jnp.sum(projected * projected, axis=0) / person_count

    def window_score(gene):
        begin = window_start[gene] - first_variant
        size = window_length[gene]

        def add_block(block, running):
            window = lax.dynamic_slice(
                score_ext, (jnp.int32(0), begin + block * step_width), (block_traits, step_width)
            )
            piece = weight_block(gene, block, size)
            return running + lax.dot_general(
                piece, window, (((1,), (1,)), ((), ())), preferred_element_type=jnp.float32
            )

        blocks_needed = (size + step_width - 1) // step_width
        return lax.fori_loop(
            0, blocks_needed, add_block, jnp.zeros((tissue_count, block_traits), jnp.float32)
        )

    empty = jnp.zeros((gene_count, tissue_count), jnp.float32)

    def every_gene(gene, partial_value):
        return partial_value.at[gene].set(window_variance(gene, window_length[gene]))

    variance = lax.fori_loop(0, gene_count, every_gene, empty)

    def score_gene(gene, partial_value):
        return partial_value.at[gene].set(window_score(gene))

    numerator = lax.fori_loop(
        0, gene_count, score_gene, jnp.zeros((gene_count, tissue_count, block_traits), jnp.float32)
    )
    return numerator / jnp.sqrt(variance + EPSILON)[:, :, None]


MESH = pl.DeviceIdType.MESH
BF16 = jnp.bfloat16
F32 = jnp.float32
Y_COUNT = 2
CHUNKS = 9


def spread_column(row):
    return jnp.transpose(jnp.broadcast_to(row, (128, 128)))


def pack_kernel(low_ref, high_ref, left_ref, slot_ref, out_ref, total, column):
    block = pl.program_id(0)
    width = out_ref.shape[2]
    depth = left_ref.shape[1] // 6
    total[...] = jnp.zeros_like(total)
    lane = (lax.broadcasted_iota(jnp.int32, (depth, 128), 1) + block * width).astype(F32)

    @pl.when(block == 0)
    def _():
        for b in range(slot_ref.shape[0]):
            column[b * 128 : (b + 1) * 128, :] = spread_column(slot_ref[b : b + 1, :])

    def add_rows(k, carry):
        start = pl.multiple_of(k * depth, depth)
        slots = column[pl.ds(start, depth), :]
        chosen = jnp.concatenate(
            [
                jnp.where(slots == lane + 128 * b, 1.0, 0.0).astype(BF16)
                for b in range(width // 128)
            ],
            axis=1,
        )
        total[...] += jnp.dot(
            left_ref[:, pl.ds(start, depth)], chosen, preferred_element_type=F32
        )
        return carry

    lax.fori_loop(low_ref[block], high_ref[block], add_rows, 0)
    out_ref[0] = total[...].astype(BF16)


def pack_rows(left, slot, low, high, stripes):
    height, rows = left.shape
    bucket = rows // stripes
    width = bucket // 3
    return pl.pallas_call(
        pack_kernel,
        grid_spec=pltpu.PrefetchScalarGridSpec(
            num_scalar_prefetch=2,
            grid=(stripes * 3,),
            in_specs=[
                pl.BlockSpec((height, rows), lambda i, lo, hi: (0, 0)),
                pl.BlockSpec(slot.shape, lambda i, lo, hi: (0, 0)),
            ],
            out_specs=pl.BlockSpec((1, height, width), lambda i, lo, hi: (i // 3, 0, i % 3)),
            scratch_shapes=[pltpu.VMEM((height, width), F32), pltpu.VMEM((rows, 128), F32)],
        ),
        out_shape=jax.ShapeDtypeStruct((stripes, height, bucket), BF16),
        cost_estimate=pl.CostEstimate(
            flops=height * rows * rows, bytes_accessed=4 * height * rows, transcendentals=0
        ),
    )(low, high, left, slot)


def combine_kernel(
    z_count,
    traits,
    got_ref,
    precision_ref,
    square_ref,
    out_ref,
    variance_ref,
    column,
    mine,
    rim,
    squares,
    own,
    y_got,
    pair,
    z_got,
    weights,
    root,
    total,
    y_send,
    y_recv,
    z_send,
    z_recv,
    w_send,
    w_recv,
    s_send,
    s_recv,
    r_send,
    r_recv,
):
    cohort = lax.axis_index("cohort")
    stripe = lax.axis_index("stripe")
    cohorts = z_count * Y_COUNT
    z, y = cohort // Y_COUNT, lax.rem(cohort, Y_COUNT)
    stripes, _, bucket = got_ref.shape
    rows = stripes * bucket
    ahead, behind = lax.rem(stripe + 1, stripes), lax.rem(stripe + stripes - 1, stripes)
    block = traits // cohorts
    width = own.shape[4]

    barrier = pltpu.get_barrier_semaphore()
    for d in range(1, cohorts):
        pl.semaphore_signal(
            barrier, inc=1, device_id=(lax.rem(cohort + d, cohorts), stripe), device_id_type=MESH
        )
    for other in (ahead, behind):
        pl.semaphore_signal(barrier, inc=1, device_id=(cohort, other), device_id_type=MESH)
    pl.semaphore_wait(barrier, cohorts + 1)

    def weight_copy(d):
        return pltpu.make_async_remote_copy(
            src_ref=precision_ref,
            dst_ref=weights.at[d],
            send_sem=w_send.at[d],
            recv_sem=w_recv.at[d],
            device_id=(lax.rem(cohort + d, cohorts), stripe),
            device_id_type=MESH,
        )

    def square_copy(d):
        return pltpu.make_async_remote_copy(
            src_ref=square_ref,
            dst_ref=squares.at[d],
            send_sem=s_send.at[d],
            recv_sem=s_recv.at[d],
            device_id=(lax.rem(cohort + d, cohorts), stripe),
            device_id_type=MESH,
        )

    def rim_copy(k):
        return pltpu.make_async_remote_copy(
            src_ref=mine.at[k],
            dst_ref=rim.at[k],
            send_sem=r_send.at[k],
            recv_sem=r_recv.at[k],
            device_id=(cohort, behind),
            device_id_type=MESH,
        )

    def y_copy(k):
        return pltpu.make_async_remote_copy(
            src_ref=own.at[k, 1 - y],
            dst_ref=y_got.at[k],
            send_sem=y_send.at[k],
            recv_sem=y_recv.at[k],
            device_id=(z * Y_COUNT + 1 - y, stripe),
            device_id_type=MESH,
        )

    def z_copy(k, d):
        other = lax.rem(z + d, z_count)
        return pltpu.make_async_remote_copy(
            src_ref=pair.at[k, other],
            dst_ref=z_got.at[k, d],
            send_sem=z_send.at[k, d],
            recv_sem=z_recv.at[k, d],
            device_id=(other * Y_COUNT + y, stripe),
            device_id_type=MESH,
        )

    for d in range(1, cohorts):
        weight_copy(d).start()
        square_copy(d).start()
    root[...] = jnp.sqrt(precision_ref[...])
    out_ref[:, 2 * rows :] = jnp.zeros((block, out_ref.shape[1] - 2 * rows), BF16)

    def spread_keys(s, carry):
        digits = got_ref[s, traits : traits + 16, :].astype(F32)
        keys = 64.0 * digits[0:1] + digits[1:2]
        for b in range(bucket // 128):
            column[pl.ds(pl.multiple_of(s * bucket + b * 128, 128), 128), :] = spread_column(
                keys[:, b * 128 : (b + 1) * 128]
            )
        return carry

    lax.fori_loop(0, stripes, spread_keys, 0)

    def step(k, carry):
        @pl.when(k < CHUNKS)
        def _():
            lane = (lax.broadcasted_iota(jnp.int32, (2 * bucket, 128), 1) + k * width).astype(F32)
            total[...] = jnp.zeros_like(total)

            def add_source(s, inner):
                keys = column[pl.ds(pl.multiple_of(2 * s * bucket, 2 * bucket), 2 * bucket), :]
                chosen = jnp.concatenate(
                    [
                        jnp.where(keys == lane + 128 * b, 1.0, 0.0).astype(BF16)
                        for b in range(width // 128)
                    ],
                    axis=1,
                )
                both = jnp.concatenate(
                    [got_ref[2 * s, :traits, :], got_ref[2 * s + 1, :traits, :]], axis=1
                )
                total[...] += jnp.dot(both, chosen, preferred_element_type=F32)
                return inner

            lax.fori_loop(0, stripes // 2, add_source, 0)
            scale = root[:, pl.ds(pl.multiple_of(k * width, width), width)]
            for c in range(cohorts):
                own[k, c % Y_COUNT, c // Y_COUNT] = (
                    total[c * block : (c + 1) * block, :] * scale
                ).astype(BF16)
            y_copy(k).start()

        @pl.when(k >= 1)
        def _():
            last = k - 1
            y_copy(last).wait_recv()
            for zi in range(z_count):
                pair[last, zi] = (
                    own[last, y, zi].astype(F32) + y_got[last, zi].astype(F32)
                ).astype(BF16)
            for d in range(1, z_count):
                z_copy(last, d).start()

        return carry

    lax.fori_loop(0, CHUNKS + 1, step, 0)

    weight_sum = precision_ref[...]
    for d in range(1, cohorts):
        weight_copy(d).wait_recv()
        weight_sum = weight_sum + weights[d]
    root[...] = jnp.sqrt(weight_sum)

    def finish(k, carry):
        summed = pair[k, z].astype(F32)
        for d in range(1, z_count):
            z_copy(k, d).wait_recv()
            summed = summed + z_got[k, d].astype(F32)
        here = pl.ds(pl.multiple_of(k * width, width), width)
        value = (summed / root[:, here]).astype(BF16)
        mine[k] = value
        out_ref[:, here] = value
        rim_copy(k).start()
        y_copy(k).wait_send()
        for d in range(1, z_count):
            z_copy(k, d).wait_send()
        return carry

    lax.fori_loop(0, CHUNKS, finish, 0)
    square_sum = square_ref[...]
    for d in range(1, cohorts):
        square_copy(d).wait_recv()
        square_sum = square_sum + squares[d]
    variance_ref[...] = square_sum

    def take_rim(k, carry):
        rim_copy(k).wait_recv()
        out_ref[:, pl.ds(pl.multiple_of(rows + k * width, width), width)] = rim[k]
        rim_copy(k).wait_send()
        return carry

    lax.fori_loop(0, CHUNKS, take_rim, 0)
    for d in range(1, cohorts):
        weight_copy(d).wait_send()
        square_copy(d).wait_send()


def combine(got, precision, squares, traits, cohorts, step):
    stripes, _, bucket = got.shape
    rows = stripes * bucket
    width = rows // CHUNKS
    block = traits // cohorts
    z_count = cohorts // Y_COUNT
    vmem = pl.BlockSpec(memory_space=pltpu.VMEM)
    dma = pltpu.SemaphoreType.DMA
    return pl.pallas_call(
        functools.partial(combine_kernel, z_count, traits),
        out_shape=[
            jax.ShapeDtypeStruct((block, 2 * rows + step), BF16),
            jax.ShapeDtypeStruct(squares.shape, F32),
        ],
        in_specs=[vmem] * 3,
        out_specs=[vmem] * 2,
        scratch_shapes=[
            pltpu.VMEM((rows, 128), F32),
            pltpu.VMEM((CHUNKS, block, width), BF16),
            pltpu.VMEM((CHUNKS, block, width), BF16),
            pltpu.VMEM((cohorts,) + squares.shape, F32),
            pltpu.VMEM((CHUNKS, Y_COUNT, z_count, block, width), BF16),
            pltpu.VMEM((CHUNKS, z_count, block, width), BF16),
            pltpu.VMEM((CHUNKS, z_count, block, width), BF16),
            pltpu.VMEM((CHUNKS, z_count, block, width), BF16),
            pltpu.VMEM((cohorts, 1, rows), F32),
            pltpu.VMEM((1, rows), F32),
            pltpu.VMEM((traits, width), F32),
            dma((CHUNKS,)),
            dma((CHUNKS,)),
            dma((CHUNKS, z_count)),
            dma((CHUNKS, z_count)),
            dma((cohorts,)),
            dma((cohorts,)),
            dma((cohorts,)),
            dma((cohorts,)),
            dma((CHUNKS,)),
            dma((CHUNKS,)),
        ],
        compiler_params=pltpu.CompilerParams(collective_id=0, has_side_effects=True),
    )(got, precision, squares)


def variance_kernel(begin_ref, size_ref, weight_ref, side_ref, square_ref, aligned_ref, total):
    group, tissues, span = weight_ref.shape
    step = span // 4
    blocks = step // 128
    lane = lax.broadcasted_iota(jnp.int32, (tissues, 128), 1)

    def one_gene(g, carry):
        gene = pl.program_id(0) * group + g
        size = size_ref[gene]
        shift = lax.rem(begin_ref[gene], 128)
        base = begin_ref[gene] - shift
        total[...] = jnp.zeros_like(total)

        def add_part(part, inner):
            first = part * blocks

            def turned(b):
                at = jnp.clip(first + b, 0, span // 128 - 1)
                piece = weight_ref[g, :, pl.ds(pl.multiple_of(at * 128, 128), 128)]
                return pltpu.roll(piece.astype(F32), shift, 1)

            before = turned(-1)
            made = []
            for b in range(blocks):
                after = turned(b)
                place = (first + b) * 128 + lane - shift
                keep = jnp.logical_and(place >= 0, place < size)
                made.append(
                    jnp.where(keep, jnp.where(lane < shift, before, after), 0.0).astype(BF16)
                )
                before = after
            made = jnp.concatenate(made, axis=1)
            aligned_ref[g, :, pl.ds(pl.multiple_of(first * 128, 128), step)] = made
            columns = side_ref[:, pl.ds(pl.multiple_of(base + first * 128, 128), step)]
            total[...] += lax.dot_general(
                columns, made, (((1,), (1,)), ((), ())), preferred_element_type=F32
            )
            return inner

        lax.fori_loop(0, (size + shift + step - 1) // step, add_part, 0)
        projected = total[...]
        square_ref[g] = jnp.sum(projected * projected, axis=0, keepdims=True)
        return carry

    lax.fori_loop(0, group, one_gene, 0)


def score_kernel(persons, begin_ref, size_ref, aligned_ref, side_ref, square_ref, out_ref, total):
    group, tissues, span = aligned_ref.shape
    step = span // 5

    def one_gene(g, carry):
        gene = pl.program_id(0) * group + g
        shift = lax.rem(begin_ref[gene], 128)
        base = begin_ref[gene] - shift
        total[...] = jnp.zeros_like(total)

        def add_part(part, inner):
            first = part * step
            total[...] += lax.dot_general(
                side_ref[:, pl.ds(pl.multiple_of(base + first, 128), step)],
                aligned_ref[g, :, pl.ds(pl.multiple_of(first, 128), step)],
                (((1,), (1,)), ((), ())),
                preferred_element_type=F32,
            )
            return inner

        lax.fori_loop(0, (size_ref[gene] + shift + step - 1) // step, add_part, 0)
        out_ref[g] = total[...] / jnp.sqrt(square_ref[g] / persons + EPSILON)
        return carry

    lax.fori_loop(0, group, one_gene, 0)


def by_gene(kernel, begin, size, weights, side, extra, outs, group):
    genes, tissues, span = weights.shape

    def rows_of(shape):
        return pl.BlockSpec((group,) + shape[1:], lambda g, b, s: (g, 0, 0))

    return pl.pallas_call(
        kernel,
        grid_spec=pltpu.PrefetchScalarGridSpec(
            num_scalar_prefetch=2,
            grid=(genes // group,),
            in_specs=[
                rows_of(weights.shape),
                pl.BlockSpec(side.shape, lambda g, b, s: (0, 0)),
            ]
            + [rows_of(e.shape) for e in extra],
            out_specs=[rows_of(o.shape) for o in outs],
            scratch_shapes=[pltpu.VMEM((side.shape[0], tissues), F32)],
        ),
        out_shape=outs,
        cost_estimate=pl.CostEstimate(
            flops=16 * genes * tissues * span * side.shape[0],
            bytes_accessed=4 * genes * tissues * span,
            transcendentals=0,
        ),
    )(begin, size, weights, side, *extra)


def extended(block, step):
    rim = passed_along(block, "stripe", -1)
    return jnp.concatenate([block, rim, jnp.zeros((block.shape[0], step), BF16)], axis=1)


def fast_device(
    cohort_scores,
    allele_match,
    allele_flip,
    precision,
    reference_panel,
    gene_weights,
    window_start,
    window_length,
):
    row_count, trait_count = cohort_scores.shape[1:]
    stripes = lax.axis_size("stripe")
    cohorts = lax.axis_size("cohort")
    bucket = row_count // stripes
    persons = reference_panel.shape[0]
    step = gene_weights.shape[2] // 4
    begin = window_start - lax.axis_index("stripe") * row_count

    share = persons // cohorts
    panel = lax.dynamic_slice_in_dim(
        reference_panel, lax.axis_index("cohort") * share, share, axis=0
    )
    panel_ext = extended(panel, step)

    match = allele_match[0]
    target = match // row_count
    inside = match - target * row_count
    member = target[None, :] == jnp.arange(stripes, dtype=jnp.int32)[:, None]
    ranking = jnp.cumsum(member.astype(jnp.int32), axis=1)
    rank = jnp.sum(jnp.where(member, ranking, 0), axis=0) - 1
    slot = target * bucket + rank
    width = bucket // 3
    depth = row_count // 6
    ends = ranking[:, depth - 1 :: depth]
    edges = jnp.arange(3, dtype=jnp.int32) * width
    low = jnp.sum(ends[:, None, :] <= edges[None, :, None], axis=2, dtype=jnp.int32)
    high = 1 + jnp.sum(ends[:, None, :] < (edges + width)[None, :, None], axis=2, dtype=jnp.int32)
    signs = (1 - 2 * allele_flip[0]).astype(BF16)
    left = jnp.concatenate(
        [
            (cohort_scores[0] * signs[:, None]).T,
            (inside // 64).astype(BF16)[None, :],
            lax.rem(inside, 64).astype(BF16)[None, :],
            jnp.zeros((14, row_count), BF16),
        ],
        axis=0,
    )
    outgoing = pack_rows(
        left,
        slot.reshape(row_count // 128, 128).astype(F32),
        low.reshape(-1),
        high.reshape(-1),
        stripes,
    )
    got = lax.all_to_all(outgoing, "stripe", split_axis=0, concat_axis=0, tiled=True)

    genes, tissues, _ = gene_weights.shape
    group = 4 if genes % 4 == 0 else 1
    squares, aligned = by_gene(
        variance_kernel,
        begin,
        window_length,
        gene_weights,
        panel_ext,
        (),
        [
            jax.ShapeDtypeStruct((genes, 1, tissues), F32),
            jax.ShapeDtypeStruct((genes, tissues, 5 * step), BF16),
        ],
        group,
    )
    score_ext, square_sums = combine(got, precision, squares, trait_count, cohorts, step)
    (association,) = by_gene(
        functools.partial(score_kernel, persons),
        begin,
        window_length,
        aligned,
        score_ext,
        (square_sums,),
        [jax.ShapeDtypeStruct((genes, score_ext.shape[0], tissues), F32)],
        group,
    )
    return jnp.transpose(association, (0, 2, 1))


def on_device(cohort_scores, *others):
    rows, traits = cohort_scores.shape[1:]
    stripes = lax.axis_size("stripe")
    cohorts = lax.axis_size("cohort")
    span = others[4].shape[2]
    fits = (
        cohorts % Y_COUNT == 0
        and traits % (16 * cohorts) == 0
        and rows % (384 * stripes) == 0
        and rows % (128 * CHUNKS) == 0
        and rows % 768 == 0
        and stripes % 2 == 0
        and rows < 16384
        and span % 512 == 0
        and span <= rows
        and others[3].shape[0] % (16 * cohorts) == 0
    )
    if fits:
        return fast_device(cohort_scores, *others)
    return general_device(cohort_scores, *others)


def solution(mesh):
    in_specs = (
        P("cohort", "stripe", None),
        P("cohort", "stripe"),
        P("cohort", "stripe"),
        P("cohort", "stripe"),
        P(None, "stripe"),
        P("stripe", None, None),
        P("stripe"),
        P("stripe"),
    )
    out_specs = P("stripe", None, "cohort")
    return jax.shard_map(
        on_device, mesh=mesh, in_specs=in_specs, out_specs=out_specs, check_vma=False
    )
```

```python
import functools

import jax
import jax.numpy as jnp
from jax import lax
from jax.experimental import pallas as pl
from jax.experimental.pallas import tpu as pltpu
from jax.sharding import PartitionSpec as P

EPSILON = 1e-06


def passed_along(block, axis, distance):
    devices = range(lax.axis_size(axis))
    route = [(i - distance, i) for i in devices if i - distance in devices]
    return lax.ppermute(block, axis, route)


def general_device(
    cohort_scores,
    allele_match,
    allele_flip,
    precision,
    reference_panel,
    gene_weights,
    window_start,
    window_length,
):
    row_count = cohort_scores.shape[1]
    trait_count = cohort_scores.shape[2]
    stripe_count = lax.axis_size("stripe")
    cohort_count = lax.axis_size("cohort")
    bucket_rows = row_count // stripe_count
    block_traits = trait_count // cohort_count
    person_count = reference_panel.shape[0]
    gene_count = gene_weights.shape[0]
    tissue_count = gene_weights.shape[1]
    window_span = gene_weights.shape[2]
    step_width = min(512, window_span)
    first_variant = lax.axis_index("stripe") * row_count
    target = allele_match[0] // row_count
    inside = allele_match[0] - target * row_count
    member = (target[:, None] == jnp.arange(stripe_count, dtype=jnp.int32)[None, :]).astype(
        jnp.int32
    )
    ranking = jnp.sum(jnp.cumsum(member, axis=0) * member, axis=1) - 1
    placing = target * bucket_rows + ranking
    signs = (1 - 2 * allele_flip[0]).astype(jnp.bfloat16)
    flipped = cohort_scores[0] * signs[:, None]
    outgoing = jnp.zeros((row_count, trait_count), jnp.bfloat16).at[placing].set(flipped)
    out_keys = jnp.zeros((row_count,), jnp.int32).at[placing].set(inside)
    got_rows, got_keys = (
        lax.all_to_all(
            outgoing.reshape(stripe_count, bucket_rows, trait_count),
            "stripe",
            split_axis=0,
            concat_axis=0,
            tiled=True,
        ),
        lax.all_to_all(
            out_keys.reshape(stripe_count, bucket_rows),
            "stripe",
            split_axis=0,
            concat_axis=0,
            tiled=True,
        ),
    )
    aligned = (
        jnp.zeros((row_count, trait_count), jnp.bfloat16)
        .at[got_keys.reshape(row_count)]
        .set(got_rows.reshape(row_count, trait_count))
    )
    own_weight = precision[0]
    weighted = (jnp.sqrt(own_weight)[:, None] * aligned).astype(jnp.bfloat16)
    total_weight = lax.psum(own_weight, "cohort")
    received = lax.all_to_all(weighted, "cohort", split_axis=1, concat_axis=1, tiled=True)
    summed = jnp.sum(
        received.reshape(row_count, cohort_count, block_traits).astype(jnp.float32), axis=1
    )
    combined = (summed.T / jnp.sqrt(total_weight)[None, :]).astype(jnp.bfloat16)
    joined = jnp.concatenate([reference_panel, combined], axis=0)
    moved = passed_along(joined, "stripe", -1)
    panel_rim = moved[:person_count]
    score_rim = moved[person_count:]
    panel_ext = jnp.concatenate([reference_panel, panel_rim], axis=1)
    score_ext = jnp.concatenate([combined, score_rim], axis=1)

    def weight_block(gene, block, size):
        offset = block * step_width
        piece = lax.dynamic_slice(
            gene_weights[gene], (jnp.int32(0), offset), (tissue_count, step_width)
        )
        keep = offset + jnp.arange(step_width, dtype=jnp.int32) < size
        return jnp.where(keep[None, :], piece, jnp.zeros_like(piece))

    def window_variance(gene, size):
        begin = window_start[gene] - first_variant

        def add_block(block, running):
            columns = lax.dynamic_slice(
                panel_ext, (jnp.int32(0), begin + block * step_width), (person_count, step_width)
            )
            piece = weight_block(gene, block, size)
            return running + lax.dot_general(
                columns, piece, (((1,), (1,)), ((), ())), preferred_element_type=jnp.float32
            )

        blocks_needed = (size + step_width - 1) // step_width
        projected = lax.fori_loop(
            0, blocks_needed, add_block, jnp.zeros((person_count, tissue_count), jnp.float32)
        )
        return jnp.sum(projected * projected, axis=0) / person_count

    def window_score(gene):
        begin = window_start[gene] - first_variant
        size = window_length[gene]

        def add_block(block, running):
            window = lax.dynamic_slice(
                score_ext, (jnp.int32(0), begin + block * step_width), (block_traits, step_width)
            )
            piece = weight_block(gene, block, size)
            return running + lax.dot_general(
                piece, window, (((1,), (1,)), ((), ())), preferred_element_type=jnp.float32
            )

        blocks_needed = (size + step_width - 1) // step_width
        return lax.fori_loop(
            0, blocks_needed, add_block, jnp.zeros((tissue_count, block_traits), jnp.float32)
        )

    empty = jnp.zeros((gene_count, tissue_count), jnp.float32)

    def every_gene(gene, partial_value):
        return partial_value.at[gene].set(window_variance(gene, window_length[gene]))

    variance = lax.fori_loop(0, gene_count, every_gene, empty)

    def score_gene(gene, partial_value):
        return partial_value.at[gene].set(window_score(gene))

    numerator = lax.fori_loop(
        0, gene_count, score_gene, jnp.zeros((gene_count, tissue_count, block_traits), jnp.float32)
    )
    return numerator / jnp.sqrt(variance + EPSILON)[:, :, None]


MESH = pl.DeviceIdType.MESH
BF16 = jnp.bfloat16
F32 = jnp.float32
Y_COUNT = 2
CHUNKS = 9


LAG = 4


def spread_column(row):
    return jnp.transpose(jnp.broadcast_to(row, (128, 128)))


def pack_kernel(low_ref, high_ref, left_ref, slot_ref, out_ref, total, column):
    block = pl.program_id(0)
    width = out_ref.shape[2]
    depth = left_ref.shape[1] // 6
    total[...] = jnp.zeros_like(total)
    lane = (lax.broadcasted_iota(jnp.int32, (depth, 128), 1) + block * width).astype(F32)

    @pl.when(block == 0)
    def _():
        for b in range(slot_ref.shape[0]):
            column[b * 128 : (b + 1) * 128, :] = spread_column(slot_ref[b : b + 1, :])

    def add_rows(k, carry):
        start = pl.multiple_of(k * depth, depth)
        slots = column[pl.ds(start, depth), :]
        chosen = jnp.concatenate(
            [
                jnp.where(slots == lane + 128 * b, 1.0, 0.0).astype(BF16)
                for b in range(width // 128)
            ],
            axis=1,
        )
        total[...] += jnp.dot(
            left_ref[:, pl.ds(start, depth)], chosen, preferred_element_type=F32
        )
        return carry

    lax.fori_loop(low_ref[block], high_ref[block], add_rows, 0)
    out_ref[0] = total[...].astype(BF16)


def pack_rows(left, slot, low, high, stripes):
    height, rows = left.shape
    bucket = rows // stripes
    width = bucket // 3
    return pl.pallas_call(
        pack_kernel,
        grid_spec=pltpu.PrefetchScalarGridSpec(
            num_scalar_prefetch=2,
            grid=(stripes * 3,),
            in_specs=[
                pl.BlockSpec((height, rows), lambda i, lo, hi: (0, 0)),
                pl.BlockSpec(slot.shape, lambda i, lo, hi: (0, 0)),
            ],
            out_specs=pl.BlockSpec((1, height, width), lambda i, lo, hi: (i // 3, 0, i % 3)),
            scratch_shapes=[pltpu.VMEM((height, width), F32), pltpu.VMEM((rows, 128), F32)],
        ),
        out_shape=jax.ShapeDtypeStruct((stripes, height, bucket), BF16),
        cost_estimate=pl.CostEstimate(
            flops=height * rows * rows, bytes_accessed=4 * height * rows, transcendentals=0
        ),
    )(low, high, left, slot)


def combine_kernel(
    z_count,
    traits,
    got_ref,
    precision_ref,
    square_ref,
    out_ref,
    variance_ref,
    column,
    mine,
    rim,
    squares,
    own,
    y_got,
    pair,
    z_got,
    weights,
    root,
    norm,
    total,
    y_send,
    y_recv,
    z_send,
    z_recv,
    w_send,
    w_recv,
    s_send,
    s_recv,
    r_send,
    r_recv,
):
    cohort = lax.axis_index("cohort")
    stripe = lax.axis_index("stripe")
    cohorts = z_count * Y_COUNT
    z, y = cohort // Y_COUNT, lax.rem(cohort, Y_COUNT)
    stripes, _, bucket = got_ref.shape
    rows = stripes * bucket
    ahead, behind = lax.rem(stripe + 1, stripes), lax.rem(stripe + stripes - 1, stripes)
    block = traits // cohorts
    width = own.shape[4]

    barrier = pltpu.get_barrier_semaphore()
    for d in range(1, cohorts):
        pl.semaphore_signal(
            barrier, inc=1, device_id=(lax.rem(cohort + d, cohorts), stripe), device_id_type=MESH
        )
    for other in (ahead, behind):
        pl.semaphore_signal(barrier, inc=1, device_id=(cohort, other), device_id_type=MESH)
    pl.semaphore_wait(barrier, cohorts + 1)

    def weight_copy(d):
        return pltpu.make_async_remote_copy(
            src_ref=precision_ref,
            dst_ref=weights.at[d],
            send_sem=w_send.at[d],
            recv_sem=w_recv.at[d],
            device_id=(lax.rem(cohort + d, cohorts), stripe),
            device_id_type=MESH,
        )

    def square_copy(d):
        return pltpu.make_async_remote_copy(
            src_ref=square_ref,
            dst_ref=squares.at[d],
            send_sem=s_send.at[d],
            recv_sem=s_recv.at[d],
            device_id=(lax.rem(cohort + d, cohorts), stripe),
            device_id_type=MESH,
        )

    def rim_copy(k):
        return pltpu.make_async_remote_copy(
            src_ref=mine.at[k],
            dst_ref=rim.at[k],
            send_sem=r_send.at[k],
            recv_sem=r_recv.at[k],
            device_id=(cohort, behind),
            device_id_type=MESH,
        )

    def y_copy(k):
        return pltpu.make_async_remote_copy(
            src_ref=own.at[k, 1 - y],
            dst_ref=y_got.at[k],
            send_sem=y_send.at[k],
            recv_sem=y_recv.at[k],
            device_id=(z * Y_COUNT + 1 - y, stripe),
            device_id_type=MESH,
        )

    def z_copy(k, d):
        other = lax.rem(z + d, z_count)
        return pltpu.make_async_remote_copy(
            src_ref=pair.at[k, other],
            dst_ref=z_got.at[k, d],
            send_sem=z_send.at[k, d],
            recv_sem=z_recv.at[k, d],
            device_id=(other * Y_COUNT + y, stripe),
            device_id_type=MESH,
        )

    for d in range(1, cohorts):
        weight_copy(d).start()
        square_copy(d).start()
    root[...] = jnp.sqrt(precision_ref[...])
    out_ref[:, 2 * rows :] = jnp.zeros((block, out_ref.shape[1] - 2 * rows), BF16)

    def spread_keys(s, carry):
        digits = got_ref[s, traits : traits + 16, :].astype(F32)
        keys = 64.0 * digits[0:1] + digits[1:2]
        for b in range(bucket // 128):
            column[pl.ds(pl.multiple_of(s * bucket + b * 128, 128), 128), :] = spread_column(
                keys[:, b * 128 : (b + 1) * 128]
            )
        return carry

    lax.fori_loop(0, stripes, spread_keys, 0)

    def step(k, carry):
        @pl.when(k < CHUNKS)
        def _():
            lane = (lax.broadcasted_iota(jnp.int32, (2 * bucket, 128), 1) + k * width).astype(F32)
            total[...] = jnp.zeros_like(total)

            def add_source(s, inner):
                keys = column[pl.ds(pl.multiple_of(2 * s * bucket, 2 * bucket), 2 * bucket), :]
                chosen = jnp.concatenate(
                    [
                        jnp.where(keys == lane + 128 * b, 1.0, 0.0).astype(BF16)
                        for b in range(width // 128)
                    ],
                    axis=1,
                )
                both = jnp.concatenate(
                    [got_ref[2 * s, :traits, :], got_ref[2 * s + 1, :traits, :]], axis=1
                )
                total[...] += jnp.dot(both, chosen, preferred_element_type=F32)
                return inner

            lax.fori_loop(0, stripes // 2, add_source, 0)
            scale = root[:, pl.ds(pl.multiple_of(k * width, width), width)]
            for c in range(cohorts):
                own[k, c % Y_COUNT, c // Y_COUNT] = (
                    total[c * block : (c + 1) * block, :] * scale
                ).astype(BF16)
            y_copy(k).start()

        @pl.when(jnp.logical_and(k >= 1, k <= CHUNKS))
        def _():
            last = k - 1
            y_copy(last).wait_recv()
            for zi in range(z_count):
                pair[last, zi] = (
                    own[last, y, zi].astype(F32) + y_got[last, zi].astype(F32)
                ).astype(BF16)
            for d in range(1, z_count):
                z_copy(last, d).start()

        @pl.when(k == LAG)
        def _():
            weight_sum = precision_ref[...]
            for d in range(1, cohorts):
                weight_copy(d).wait_recv()
                weight_sum = weight_sum + weights[d]
            norm[...] = jnp.sqrt(weight_sum)

        @pl.when(k >= LAG)
        def _():
            done = k - LAG
            summed = pair[done, z].astype(F32)
            for d in range(1, z_count):
                z_copy(done, d).wait_recv()
                summed = summed + z_got[done, d].astype(F32)
            here = pl.ds(pl.multiple_of(done * width, width), width)
            value = (summed / norm[:, here]).astype(BF16)
            mine[done] = value
            out_ref[:, here] = value
            rim_copy(done).start()
            y_copy(done).wait_send()
            for d in range(1, z_count):
                z_copy(done, d).wait_send()

        return carry

    lax.fori_loop(0, CHUNKS + LAG, step, 0)
    square_sum = square_ref[...]
    for d in range(1, cohorts):
        square_copy(d).wait_recv()
        square_sum = square_sum + squares[d]
    variance_ref[...] = square_sum

    def take_rim(k, carry):
        rim_copy(k).wait_recv()
        out_ref[:, pl.ds(pl.multiple_of(rows + k * width, width), width)] = rim[k]
        rim_copy(k).wait_send()
        return carry

    lax.fori_loop(0, CHUNKS, take_rim, 0)
    for d in range(1, cohorts):
        weight_copy(d).wait_send()
        square_copy(d).wait_send()


def combine(got, precision, squares, traits, cohorts, step):
    stripes, _, bucket = got.shape
    rows = stripes * bucket
    width = rows // CHUNKS
    block = traits // cohorts
    z_count = cohorts // Y_COUNT
    vmem = pl.BlockSpec(memory_space=pltpu.VMEM)
    dma = pltpu.SemaphoreType.DMA
    return pl.pallas_call(
        functools.partial(combine_kernel, z_count, traits),
        out_shape=[
            jax.ShapeDtypeStruct((block, 2 * rows + step), BF16),
            jax.ShapeDtypeStruct(squares.shape, F32),
        ],
        in_specs=[vmem] * 3,
        out_specs=[vmem] * 2,
        scratch_shapes=[
            pltpu.VMEM((rows, 128), F32),
            pltpu.VMEM((CHUNKS, block, width), BF16),
            pltpu.VMEM((CHUNKS, block, width), BF16),
            pltpu.VMEM((cohorts,) + squares.shape, F32),
            pltpu.VMEM((CHUNKS, Y_COUNT, z_count, block, width), BF16),
            pltpu.VMEM((CHUNKS, z_count, block, width), BF16),
            pltpu.VMEM((CHUNKS, z_count, block, width), BF16),
            pltpu.VMEM((CHUNKS, z_count, block, width), BF16),
            pltpu.VMEM((cohorts, 1, rows), F32),
            pltpu.VMEM((1, rows), F32),
            pltpu.VMEM((1, rows), F32),
            pltpu.VMEM((traits, width), F32),
            dma((CHUNKS,)),
            dma((CHUNKS,)),
            dma((CHUNKS, z_count)),
            dma((CHUNKS, z_count)),
            dma((cohorts,)),
            dma((cohorts,)),
            dma((cohorts,)),
            dma((cohorts,)),
            dma((CHUNKS,)),
            dma((CHUNKS,)),
        ],
        compiler_params=pltpu.CompilerParams(collective_id=0, has_side_effects=True),
    )(got, precision, squares)


def variance_kernel(begin_ref, size_ref, weight_ref, side_ref, square_ref, aligned_ref, total):
    group, tissues, span = weight_ref.shape
    step = span // 4
    blocks = step // 128
    lane = lax.broadcasted_iota(jnp.int32, (tissues, 128), 1)

    def one_gene(g, carry):
        gene = pl.program_id(0) * group + g
        size = size_ref[gene]
        shift = lax.rem(begin_ref[gene], 128)
        base = begin_ref[gene] - shift
        total[...] = jnp.zeros_like(total)

        def add_part(part, inner):
            first = part * blocks

            def turned(b):
                at = jnp.clip(first + b, 0, span // 128 - 1)
                piece = weight_ref[g, :, pl.ds(pl.multiple_of(at * 128, 128), 128)]
                return pltpu.roll(piece.astype(F32), shift, 1)

            before = turned(-1)
            made = []
            for b in range(blocks):
                after = turned(b)
                place = (first + b) * 128 + lane - shift
                keep = jnp.logical_and(place >= 0, place < size)
                made.append(
                    jnp.where(keep, jnp.where(lane < shift, before, after), 0.0).astype(BF16)
                )
                before = after
            made = jnp.concatenate(made, axis=1)
            aligned_ref[g, :, pl.ds(pl.multiple_of(first * 128, 128), step)] = made
            columns = side_ref[:, pl.ds(pl.multiple_of(base + first * 128, 128), step)]
            total[...] += lax.dot_general(
                columns, made, (((1,), (1,)), ((), ())), preferred_element_type=F32
            )
            return inner

        lax.fori_loop(0, (size + shift + step - 1) // step, add_part, 0)
        projected = total[...]
        square_ref[g] = jnp.sum(projected * projected, axis=0, keepdims=True)
        return carry

    lax.fori_loop(0, group, one_gene, 0)


def score_kernel(persons, begin_ref, size_ref, aligned_ref, side_ref, square_ref, out_ref, total):
    group, tissues, span = aligned_ref.shape
    step = span // 5

    def one_gene(g, carry):
        gene = pl.program_id(0) * group + g
        shift = lax.rem(begin_ref[gene], 128)
        base = begin_ref[gene] - shift
        total[...] = jnp.zeros_like(total)

        def add_part(part, inner):
            first = part * step
            total[...] += lax.dot_general(
                side_ref[:, pl.ds(pl.multiple_of(base + first, 128), step)],
                aligned_ref[g, :, pl.ds(pl.multiple_of(first, 128), step)],
                (((1,), (1,)), ((), ())),
                preferred_element_type=F32,
            )
            return inner

        lax.fori_loop(0, (size_ref[gene] + shift + step - 1) // step, add_part, 0)
        out_ref[g] = total[...] / jnp.sqrt(square_ref[g] / persons + EPSILON)
        return carry

    lax.fori_loop(0, group, one_gene, 0)


def by_gene(kernel, begin, size, weights, side, extra, outs, group):
    genes, tissues, span = weights.shape

    def rows_of(shape):
        return pl.BlockSpec((group,) + shape[1:], lambda g, b, s: (g, 0, 0))

    return pl.pallas_call(
        kernel,
        grid_spec=pltpu.PrefetchScalarGridSpec(
            num_scalar_prefetch=2,
            grid=(genes // group,),
            in_specs=[
                rows_of(weights.shape),
                pl.BlockSpec(side.shape, lambda g, b, s: (0, 0)),
            ]
            + [rows_of(e.shape) for e in extra],
            out_specs=[rows_of(o.shape) for o in outs],
            scratch_shapes=[pltpu.VMEM((side.shape[0], tissues), F32)],
        ),
        out_shape=outs,
        cost_estimate=pl.CostEstimate(
            flops=16 * genes * tissues * span * side.shape[0],
            bytes_accessed=4 * genes * tissues * span,
            transcendentals=0,
        ),
    )(begin, size, weights, side, *extra)


def extended(block, step):
    rim = passed_along(block, "stripe", -1)
    return jnp.concatenate([block, rim, jnp.zeros((block.shape[0], step), BF16)], axis=1)


def fast_device(
    cohort_scores,
    allele_match,
    allele_flip,
    precision,
    reference_panel,
    gene_weights,
    window_start,
    window_length,
):
    row_count, trait_count = cohort_scores.shape[1:]
    stripes = lax.axis_size("stripe")
    cohorts = lax.axis_size("cohort")
    bucket = row_count // stripes
    persons = reference_panel.shape[0]
    step = gene_weights.shape[2] // 4
    begin = window_start - lax.axis_index("stripe") * row_count

    share = persons // cohorts
    panel = lax.dynamic_slice_in_dim(
        reference_panel, lax.axis_index("cohort") * share, share, axis=0
    )
    panel_ext = extended(panel, step)

    match = allele_match[0]
    target = match // row_count
    inside = match - target * row_count
    member = target[None, :] == jnp.arange(stripes, dtype=jnp.int32)[:, None]
    ranking = jnp.cumsum(member.astype(jnp.int32), axis=1)
    rank = jnp.sum(jnp.where(member, ranking, 0), axis=0) - 1
    slot = target * bucket + rank
    width = bucket // 3
    depth = row_count // 6
    ends = ranking[:, depth - 1 :: depth]
    edges = jnp.arange(3, dtype=jnp.int32) * width
    low = jnp.sum(ends[:, None, :] <= edges[None, :, None], axis=2, dtype=jnp.int32)
    high = 1 + jnp.sum(ends[:, None, :] < (edges + width)[None, :, None], axis=2, dtype=jnp.int32)
    signs = (1 - 2 * allele_flip[0]).astype(BF16)
    left = jnp.concatenate(
        [
            (cohort_scores[0] * signs[:, None]).T,
            (inside // 64).astype(BF16)[None, :],
            lax.rem(inside, 64).astype(BF16)[None, :],
            jnp.zeros((14, row_count), BF16),
        ],
        axis=0,
    )
    outgoing = pack_rows(
        left,
        slot.reshape(row_count // 128, 128).astype(F32),
        low.reshape(-1),
        high.reshape(-1),
        stripes,
    )
    got = lax.all_to_all(outgoing, "stripe", split_axis=0, concat_axis=0, tiled=True)

    genes, tissues, _ = gene_weights.shape
    group = 4 if genes % 4 == 0 else 1
    squares, aligned = by_gene(
        variance_kernel,
        begin,
        window_length,
        gene_weights,
        panel_ext,
        (),
        [
            jax.ShapeDtypeStruct((genes, 1, tissues), F32),
            jax.ShapeDtypeStruct((genes, tissues, 5 * step), BF16),
        ],
        group,
    )
    score_ext, square_sums = combine(got, precision, squares, trait_count, cohorts, step)
    (association,) = by_gene(
        functools.partial(score_kernel, persons),
        begin,
        window_length,
        aligned,
        score_ext,
        (square_sums,),
        [jax.ShapeDtypeStruct((genes, score_ext.shape[0], tissues), F32)],
        group,
    )
    return jnp.transpose(association, (0, 2, 1))


def on_device(cohort_scores, *others):
    rows, traits = cohort_scores.shape[1:]
    stripes = lax.axis_size("stripe")
    cohorts = lax.axis_size("cohort")
    span = others[4].shape[2]
    fits = (
        cohorts % Y_COUNT == 0
        and traits % (16 * cohorts) == 0
        and rows % (384 * stripes) == 0
        and rows % (128 * CHUNKS) == 0
        and rows % 768 == 0
        and stripes % 2 == 0
        and rows < 16384
        and span % 512 == 0
        and span <= rows
        and others[3].shape[0] % (16 * cohorts) == 0
    )
    if fits:
        return fast_device(cohort_scores, *others)
    return general_device(cohort_scores, *others)


def solution(mesh):
    in_specs = (
        P("cohort", "stripe", None),
        P("cohort", "stripe"),
        P("cohort", "stripe"),
        P("cohort", "stripe"),
        P(None, "stripe"),
        P("stripe", None, None),
        P("stripe"),
        P("stripe"),
    )
    out_specs = P("stripe", None, "cohort")
    return jax.shard_map(
        on_device, mesh=mesh, in_specs=in_specs, out_specs=out_specs, check_vma=False
    )
```
